32 devices in a mesh: parts: 2 (over y), clip: 4 (over x, core), tensor: 4 (over z).
Axes of the slice: x: 2, y: 2, z: 4, core: 2. Of those that a mesh axis runs over, the one named last changes fastest.
Arguments:
- clips: bfloat16 [32, 128, 4096], P(('parts', 'clip'), None, 'tensor'), parts along dimension 0, may hold values from -6 to 6
- targets: bfloat16 [32, 128, 4096], P(('parts', 'clip'), None, 'tensor'), parts along dimension 0, may hold values from -6 to 6
- lengths: int32 [32], P(('parts', 'clip')), parts along dimension 0, may hold values from 32 to 128, as said below
- gate_weight: bfloat16 [4096, 7168], P(None, 'tensor'), may hold values from -0.09375 to 0.09375
- up_weight: bfloat16 [4096, 7168], P(None, 'tensor'), may hold values from -0.09375 to 0.09375
- down_weight: bfloat16 [7168, 4096], P('tensor'), may hold values from -0.0625 to 0.0625
- proj_in: bfloat16 [64, 7168], P(None, 'tensor'), may hold values from -0.0625 to 0.0625
- proj_out: bfloat16 [64, 4096], replicated, may hold values from -0.09375 to 0.09375
- inv_hessian: bfloat16 [4096, 4096], P('clip', 'tensor'), may hold values from -0.2 to 2.2, as said below
- test_sketches: bfloat16 [4096, 4096], P('clip', 'tensor'), may hold values from -6 to 6
Outputs:
- scores: float32 [32, 4096], P(('parts', 'clip'), 'tensor'), parts along dimension 0
The draws below stay inside these ranges and needn't reach their ends.
There are 2 independent parts, one for each index of `parts`. The reference program is written for one: setup_inputs(seed, part) draws one part's arguments, and reference() takes and returns one part's arrays. A program takes and returns all parts, laid end to end along the dimension named above; an argument that names none is the same for every part. Nothing has to cross between parts.
Inputs may be any that keep to these rules, and one draw needn't show every extreme that they name: `lengths`: every clip has between 32 and 128 valid tokens; in each part one clip has exactly 128 and another exactly 32. `inv_hessian`: the same matrix in both parts.
All inputs are finite; a program needn't handle non-finite values.
Results may differ from the reference program's by a relative error of at most 0.0066.
Values may be sent and summed in bfloat16 or wider, within the bound.
A program may use at most 192 MiB of HBM per device.

```python
import math
import jax
import jax.numpy as jnp
from jax import lax

D = 4096
FF = 7168
PROJ = 64
FEAT = 4096
NTEST = 4096
LEN = 128
CLIPS = 16


def draw_lengths(key, part):
    first_key, second_key = jax.random.split(key)
    counts = jax.random.randint(first_key, (CLIPS,), LEN // 4, LEN + 1)
    chosen = jax.random.randint(second_key, (), 0, CLIPS)
    places = jnp.arange(CLIPS)
    counts = jnp.where(places == chosen, LEN, counts)
    counts = jnp.where(places == (chosen + 1) % CLIPS, LEN // 4, counts)
    return counts.astype(jnp.int32)


def draw_inv_hessian(key, part):
    first_key, second_key = jax.random.split(key)
    spread = jax.random.truncated_normal(first_key, -5.0, 5.0, (FEAT, FEAT), jnp.float32) * 0.02
    diag_vals = jnp.exp(jax.random.uniform(second_key, (FEAT,), jnp.float32, math.log(0.5), math.log(2.0)))
    places = jnp.arange(FEAT)
    on_diag = places[:, None] == places[None, :]
    return jnp.where(on_diag, diag_vals[None, :], spread).astype(jnp.bfloat16)


def block_scale(own_key, dims, cuts, smallest, high):
    gain = 1.0
    for dim, parts in cuts:
        steps = jax.random.uniform(jax.random.fold_in(jax.random.fold_in(own_key, 6), dim), (parts,), jnp.float32, smallest / len(cuts), high / len(cuts))
        gain = gain * jnp.repeat(jnp.exp(steps), dims[dim] // parts).reshape((-1,) + (1,) * (len(dims) - 1 - dim))
    return gain


def centred(stream_key, shape, scale, most, cuts=(), kind=jnp.bfloat16):
    array = jax.random.normal(stream_key, shape, jnp.float32) * scale
    if len(cuts) > 0:
        array = block_scale(stream_key, shape, cuts, -0.22, 0.18) * array
    return jnp.clip(array, min=-most, max=most).astype(kind)


def setup_inputs(seed: int = 0, part: int = 0) -> dict:
    keys = jax.random.split(jax.random.key(seed), 11)
    own_keys = jax.random.split(jax.random.fold_in(keys[10], part), 11)
    return {
        "clips": centred(own_keys[0], (CLIPS, LEN, D), 1.0, 6.0, ((0, 4), (2, 4))),
        "targets": centred(own_keys[1], (CLIPS, LEN, D), 1.0, 6.0, ((0, 4), (2, 4))),
        "lengths": draw_lengths(jax.random.fold_in(jax.random.fold_in(keys[10], part), 71), part),
        "gate_weight": centred(keys[3], (D, FF), D ** -0.5, 0.09375, ((1, 4),)),
        "up_weight": centred(keys[4], (D, FF), D ** -0.5, 0.09375, ((1, 4),)),
        "down_weight": centred(keys[5], (FF, D), FF ** -0.5, 0.0625, ((0, 4),)),
        "proj_in": centred(keys[6], (PROJ, FF), FF ** -0.5, 0.0625, ((1, 4),)),
        "proj_out": centred(keys[7], (PROJ, D), D ** -0.5, 0.09375),
        "inv_hessian": draw_inv_hessian(jax.random.fold_in(keys[10], 71), part),
        "test_sketches": centred(keys[9], (NTEST, FEAT), 1.0, 6.0, ((0, 4), (1, 4))),
    }


def reference(clips, targets, lengths, gate_weight, up_weight, down_weight, proj_in, proj_out, inv_hessian, test_sketches):
    def one_clip(items):
        tokens, golden, valid = items
        gate = jnp.dot(tokens, gate_weight, preferred_element_type=jnp.float32)
        upward = jnp.dot(tokens, up_weight, preferred_element_type=jnp.float32)
        hidden = (jax.nn.silu(gate) * upward).astype(jnp.bfloat16)
        output = jnp.dot(hidden, down_weight, preferred_element_type=jnp.float32)
        position = jnp.arange(LEN, dtype=jnp.int32)
        weight = jnp.where(position < valid, 1.0, 0.0).astype(jnp.float32) / valid.astype(jnp.float32)
        differ = jnp.clip(output - golden.astype(jnp.float32), -1.0, 1.0)
        grad_out = (differ * weight[:, None]).astype(jnp.bfloat16)
        left = jnp.dot(hidden, proj_in.T, preferred_element_type=jnp.float32)
        right = jnp.dot(grad_out, proj_out.T, preferred_element_type=jnp.float32)
        sketch = jnp.dot(left.T, right, precision=lax.Precision.HIGHEST)
        return sketch.reshape(FEAT)

    sketches = lax.map(one_clip, (clips, targets, lengths)).astype(jnp.bfloat16)
    precond = jnp.dot(sketches, inv_hessian, preferred_element_type=jnp.float32).astype(jnp.bfloat16)
    return jnp.dot(precond, test_sketches.T, preferred_element_type=jnp.float32)
```

```python
import functools

import jax
import jax.numpy as jnp
from jax import lax
from jax.experimental import pallas as pl
from jax.experimental.pallas import tpu as pltpu
from jax.sharding import PartitionSpec as P

MESH = pl.DeviceIdType.MESH
BF16, F32 = jnp.bfloat16, jnp.float32


def wait_for(ref, sem):
    pltpu.make_async_copy(ref, ref, sem).wait()


def scores_kernel(
    nc,
    n,
    chunks,
    pieces,
    tile,
    ahead,
    clips_hbm,
    targets_hbm,
    lengths_ref,
    gate_hbm,
    up_hbm,
    down_hbm,
    pin_hbm,
    pout_hbm,
    hessian_hbm,
    tests_hbm,
    out_ref,
    clips_ref,
    targets_ref,
    pin_raw,
    pin_ref,
    pout_ref,
    gate_ref,
    up_ref,
    down_ref,
    tok,
    slots,
    hid,
    joined,
    parts,
    factor,
    landed_factor,
    blocks_out,
    landed_sketch,
    partial,
    landed_partial,
    blocks,
    landed_blocks,
    load_sem,
    ag_send,
    ag_recv,
    rs_send,
    rs_recv,
    own_send,
    own_recv,
    fa_send,
    fa_recv,
    sk_send,
    sk_recv,
    pp_send,
    pp_recv,
    bl_send,
    bl_recv,
):
    my_clip = lax.axis_index("clip")
    me = lax.axis_index("tensor")
    last = n - 1
    count = lengths_ref.shape[0]
    slots_all, width = targets_ref.shape
    clip_rows = slots_all // count
    rows = hid.shape[1]
    hidden_part = gate_ref.shape[1]
    proj = pin_hbm.shape[0]
    piece_w = width // pieces
    tile_w = slots.shape[-1]
    tiles = width // tile_w
    micro = chunks * pieces
    depth, columns = hessian_hbm.shape
    tests_part = tests_hbm.shape[0]
    out_width = out_ref.shape[1]
    ratio = n // nc
    per_block = depth // (2 * proj)

    load_clips = pltpu.make_async_copy(clips_hbm, clips_ref, load_sem.at[0])
    load_clips.start()
    loads = [
        pltpu.make_async_copy(pin_hbm, pin_raw, load_sem.at[1]),
        pltpu.make_async_copy(gate_hbm, gate_ref, load_sem.at[2]),
        pltpu.make_async_copy(up_hbm, up_ref, load_sem.at[3]),
        pltpu.make_async_copy(down_hbm, down_ref, load_sem.at[4]),
        pltpu.make_async_copy(
            pout_hbm.at[:, pl.ds(pl.multiple_of(me * width, width), width)],
            pout_ref.at[pl.ds(proj, proj)],
            load_sem.at[5],
        ),
        pltpu.make_async_copy(targets_hbm, targets_ref, load_sem.at[6]),
    ]
    hessian_ref = gate_ref.at[pl.ds(0, depth), pl.ds(0, columns)]
    tests_ref = up_ref.at[pl.ds(0, tests_part), pl.ds(0, columns)]
    load_hessian = pltpu.make_async_copy(hessian_hbm, hessian_ref, load_sem.at[7])
    load_tests = pltpu.make_async_copy(tests_hbm, tests_ref, load_sem.at[8])

    barrier = pltpu.get_barrier_semaphore()

    @pl.loop(0, nc)
    def _(c):
        @pl.loop(0, n)
        def _(z):
            @pl.when((c != my_clip) | (z != me))
            def _():
                pl.semaphore_signal(
                    barrier, inc=1, device_id={"clip": c, "tensor": z}, device_id_type=MESH
                )

    pin_ref[proj:, :] = jnp.zeros((proj, hidden_part), BF16)
    pout_ref[:proj, :] = jnp.zeros((proj, width), BF16)

    ends = []
    running = jnp.int32(0)
    for c in range(count):
        running = running + lengths_ref[c]
        ends.append(running)

    def place(k, shape):
        return k * rows + lax.broadcasted_iota(jnp.int32, shape, 0)

    def pick(k):
        shape = (rows, slots_all)
        row = place(k, shape)
        source = row
        for c in range(count - 1):
            shift = clip_rows - lengths_ref[c]
            source = source + jnp.where(row >= ends[c], shift, 0)
        column = lax.broadcasted_iota(jnp.int32, shape, 1)
        hit = (column == source) & (row < ends[-1])
        return jnp.where(hit, 1.0, 0.0).astype(BF16)

    def pack_own(k):
        chosen = pick(k)
        for p in range(pieces):
            tok[k * pieces + p, me] = jnp.dot(
                chosen,
                clips_ref[:, p * piece_w : (p + 1) * piece_w],
                preferred_element_type=F32,
            ).astype(BF16)

    load_clips.wait()
    pack_own(0)
    for load in loads:
        load.start()
    pl.semaphore_wait(barrier, nc * n - 1)

    def token_copy(side, m, j):
        target = me + 1 if side == 0 else me - 1
        return pltpu.make_async_remote_copy(
            src_ref=tok.at[m, j],
            dst_ref=tok.at[m, j],
            send_sem=ag_send.at[side, m, j],
            recv_sem=ag_recv.at[m, j],
            device_id={"tensor": target},
            device_id_type=MESH,
        )

    def sum_copy(side, k, d, t):
        if side == 0:
            target, slot = me + 1, d
        else:
            target = me - 1
            slot = jnp.where(d == me - 1, n, d)
        return pltpu.make_async_remote_copy(
            src_ref=slots.at[k, d, t],
            dst_ref=slots.at[k, slot, t],
            send_sem=rs_send.at[k, d, t],
            recv_sem=rs_recv.at[k, slot, t],
            device_id={"tensor": target},
            device_id_type=MESH,
        )

    def send_own(m):
        @pl.when(me < last)
        def _():
            token_copy(0, m, me).start()

        @pl.when(me > 0)
        def _():
            token_copy(1, m, me).start()

    def gather_step(m):
        @pl.loop(1, n)
        def _(h):
            q = m - h

            @pl.when((q >= 0) & (q < micro))
            def _():
                @pl.when(me - h >= 0)
                def _():
                    wait_for(tok.at[q, me - h], ag_recv.at[q, me - h])

                    @pl.when(me < last)
                    def _():
                        token_copy(0, q, me - h).start()

                @pl.when(me + h <= last)
                def _():
                    wait_for(tok.at[q, me + h], ag_recv.at[q, me + h])

                    @pl.when(me > 0)
                    def _():
                        token_copy(1, q, me + h).start()

        @pl.when(m + ahead < micro)
        def _():
            send_own(m + ahead)

    def partial_tile(k, d, t):
        start = pl.multiple_of(d * width + t * tile_w, tile_w)
        return jnp.dot(hid[k], down_ref[:, pl.ds(start, tile_w)], preferred_element_type=F32)

    def add_and_send(side, k, d):
        first = me == (0 if side == 0 else last)

        @pl.loop(0, tiles)
        def _(t):
            @pl.when(first)
            def _():
                slots[k, d, t] = partial_tile(k, d, t).astype(BF16)

            @pl.when(jnp.logical_not(first))
            def _():
                mine = partial_tile(k, d, t)
                wait_for(slots.at[k, d, t], rs_recv.at[k, d, t])
                slots[k, d, t] = (mine + slots[k, d, t].astype(F32)).astype(BF16)

            sum_copy(side, k, d, t).start()

    def hidden_tile(k, t):
        cols = pl.ds(pl.multiple_of(t * tile, tile), tile)
        gate_act = jnp.zeros((rows, tile), F32)
        up_act = jnp.zeros((rows, tile), F32)
        for j in range(n):
            for p in range(pieces):
                piece = tok[k * pieces + p, j]
                part = slice((j * pieces + p) * piece_w, (j * pieces + p + 1) * piece_w)
                gate_act += jnp.dot(piece, gate_ref[part, cols], preferred_element_type=F32)
                up_act += jnp.dot(piece, up_ref[part, cols], preferred_element_type=F32)
        silu = gate_act / (1.0 + jnp.exp(-gate_act))
        hid[k, :, cols] = (silu * up_act).astype(BF16)

    def join_left(k):
        joined[k] = lax.dot_general(
            hid[k], pin_ref[...], (((1,), (1,)), ((), ())), preferred_element_type=F32
        )

    def part_copy(k):
        return pltpu.make_async_remote_copy(
            src_ref=joined.at[k],
            dst_ref=parts.at[me],
            send_sem=own_send.at[k],
            recv_sem=own_recv.at[me],
            device_id={"tensor": k},
            device_id_type=MESH,
        )

    def finish(k):
        shape = (rows, tile_w)
        has_left = jnp.full(shape, jnp.where(me > 0, 1.0, 0.0), F32) > 0.5
        has_right = jnp.full(shape, jnp.where(me < last, 1.0, 0.0), F32) > 0.5
        row = place(k, shape)
        length = jnp.full(shape, lengths_ref[0], jnp.int32)
        for c in range(1, count):
            length = jnp.where(row >= ends[c - 1], lengths_ref[c], length)
        weight = jnp.where(row < ends[-1], 1.0 / length.astype(F32), 0.0)
        chosen = pick(k)

        @pl.loop(0, tiles)
        def _(t):
            cols = pl.ds(pl.multiple_of(t * tile_w, tile_w), tile_w)
            total = partial_tile(k, me, t)
            golden = jnp.dot(chosen, targets_ref[:, cols], preferred_element_type=F32)

            @pl.when(me > 0)
            def _():
                wait_for(slots.at[k, me, t], rs_recv.at[k, me, t])

            @pl.when(me < last)
            def _():
                wait_for(slots.at[k, n, t], rs_recv.at[k, n, t])

            total += jnp.where(has_left, slots[k, me, t].astype(F32), 0.0)
            total += jnp.where(has_right, slots[k, n, t].astype(F32), 0.0)
            differ = jnp.clip(total - golden, -1.0, 1.0)
            grad = (differ * weight).astype(BF16)
            joined[k] += lax.dot_general(
                grad, pout_ref[:, cols], (((1,), (1,)), ((), ())), preferred_element_type=F32
            )

        @pl.when(me != k)
        def _():
            part_copy(k).start()

    @pl.loop(0, ahead)
    def _(m):
        @pl.when(m < pieces)
        def _():
            send_own(m)

    @pl.loop(1, chunks)
    def _(k):
        pack_own(k)

    @pl.loop(pieces, ahead)
    def _(m):
        send_own(m)

    @pl.loop(0, pieces + last)
    def _(m):
        gather_step(m)

    loads[0].wait()
    order_row = lax.broadcasted_iota(jnp.int32, (proj, proj), 0)
    order_col = lax.broadcasted_iota(jnp.int32, (proj, proj), 1)
    half = proj // 2
    wanted = jnp.where(order_row < half, 2 * order_row, 2 * (order_row - half) + 1)
    shuffle = jnp.where(order_col == wanted, 1.0, 0.0).astype(BF16)
    pin_ref[:proj, :] = jnp.dot(shuffle, pin_raw[...], preferred_element_type=F32).astype(BF16)

    hidden_tiles = hidden_part // tile
    middle = hidden_tiles // 2

    @pl.loop(0, chunks + last)
    def _(k):
        base = (k + 1) * pieces + last

        def more(i):
            @pl.when(base + i < micro + last)
            def _():
                gather_step(base + i)

        @pl.when(k == 0)
        def _():
            loads[1].wait()
            loads[2].wait()

        @pl.when(k < chunks)
        def _():
            @pl.loop(0, hidden_tiles)
            def _(t):
                hidden_tile(k, t)

            join_left(k)

        @pl.when(k == chunks - 1)
        def _():
            load_hessian.start()
            load_tests.start()

        @pl.when(k == 0)
        def _():
            for load in loads[3:]:
                load.wait()

        more(0)
        k_right = k - me

        @pl.when((k_right >= 0) & (k_right < chunks))
        def _():
            @pl.loop(0, last - me)
            def _(i):
                add_and_send(0, k_right, last - i)

        k_left = k - (last - me)

        @pl.when((k_left >= 0) & (k_left < chunks))
        def _():
            @pl.loop(0, me)
            def _(d):
                add_and_send(1, k_left, d)

        k_end = k - last

        @pl.when((k_end >= 0) & (k_end < chunks))
        def _():
            finish(k_end)

        for i in range(1, pieces):
            more(i)

    def factor_copy(c):
        return pltpu.make_async_remote_copy(
            src_ref=factor.at[c],
            dst_ref=landed_factor.at[me],
            send_sem=fa_send.at[c],
            recv_sem=fa_recv.at[me],
            device_id={"tensor": c},
            device_id_type=MESH,
        )

    @pl.when(me < chunks)
    def _():
        parts[me] = joined[me]

        @pl.loop(0, n)
        def _(j):
            @pl.when(j != me)
            def _():
                wait_for(parts.at[j], own_recv.at[j])

        total = parts[0]
        for j in range(1, n):
            total += parts[j]
        shape = (rows, 2 * proj)
        lane = lax.broadcasted_iota(jnp.int32, shape, 1)
        right = jnp.where(lane < proj, pltpu.roll(total, proj, 1), total)
        row = place(me, shape)
        masked = []
        for c in range(count):
            inside = row < ends[c]
            if c > 0:
                inside = inside & (row >= ends[c - 1])
            masked.append(jnp.where(inside, right, 0.0))
        product = jnp.dot(
            total.T,
            jnp.concatenate(masked, axis=1),
            precision=lax.Precision.HIGHEST,
            preferred_element_type=F32,
        )
        low = lax.broadcasted_iota(jnp.int32, (half, 2 * proj), 1) < proj
        for c in range(count):
            block = product[:, c * 2 * proj : (c + 1) * 2 * proj]
            factor[c] = jnp.where(low, block[:half], block[half:proj])

        @pl.loop(0, count)
        def _(c):
            @pl.when(c != me)
            def _():
                factor_copy(c).start()

    def sketch_copy(c, z):
        return pltpu.make_async_remote_copy(
            src_ref=blocks_out.at[c],
            dst_ref=landed_sketch.at[my_clip * count + me],
            send_sem=sk_send.at[c, z],
            recv_sem=sk_recv.at[my_clip * count + me],
            device_id={"clip": c, "tensor": z},
            device_id_type=MESH,
        )

    def every_other(act):
        @pl.loop(0, nc)
        def _(c):
            @pl.loop(0, n)
            def _(z):
                @pl.when((c != my_clip) | (z != me))
                def _():
                    act(c, z)

    @pl.when(me < count)
    def _():
        @pl.when(me < chunks)
        def _():
            landed_factor[me] = factor[me]

        @pl.loop(0, chunks)
        def _(k):
            @pl.when(k != me)
            def _():
                wait_for(landed_factor.at[k], fa_recv.at[k])

        total = landed_factor[0]
        for k in range(1, chunks):
            total += landed_factor[k]
        total = total.astype(BF16).astype(F32)
        for c in range(nc):
            blocks_out[c] = total[c * per_block : (c + 1) * per_block]
        every_other(lambda c, z: sketch_copy(c, z).start())
        landed_sketch[my_clip * count + me] = blocks_out[my_clip]

    @pl.loop(0, nc)
    def _(c):
        @pl.loop(0, count)
        def _(z):
            @pl.when((c != my_clip) | (z != me))
            def _():
                wait_for(landed_sketch.at[c * count + z], sk_recv.at[c * count + z])

    def partial_copy(c):
        return pltpu.make_async_remote_copy(
            src_ref=partial,
            dst_ref=landed_partial.at[my_clip],
            send_sem=pp_send.at[c],
            recv_sem=pp_recv.at[my_clip],
            device_id={"clip": c, "tensor": me},
            device_id_type=MESH,
        )

    def block_copy(c, q):
        return pltpu.make_async_remote_copy(
            src_ref=blocks.at[c, q],
            dst_ref=landed_blocks.at[me],
            send_sem=bl_send.at[c, q],
            recv_sem=bl_recv.at[me],
            device_id={"clip": c, "tensor": my_clip * ratio + q},
            device_id_type=MESH,
        )

    def other_clips(act):
        @pl.loop(0, nc)
        def _(c):
            @pl.when(c != my_clip)
            def _():
                act(c)

    load_hessian.wait()
    stacked = jnp.concatenate([landed_sketch[:, r, :] for r in range(per_block)], axis=1)
    partial[...] = jnp.dot(
        stacked.astype(BF16), hessian_ref[...], preferred_element_type=F32
    )
    other_clips(lambda c: partial_copy(c).start())
    landed_partial[my_clip] = partial[...]
    load_tests.wait()
    other_clips(lambda c: wait_for(landed_partial.at[c], pp_recv.at[c]))
    precond = landed_partial[0]
    for c in range(1, nc):
        precond += landed_partial[c]
    scores = lax.dot_general(
        precond.astype(BF16),
        tests_ref[...],
        (((1,), (1,)), ((), ())),
        preferred_element_type=F32,
    )
    for c in range(nc):
        for q in range(ratio):
            blocks[c, q] = scores[
                c * count : (c + 1) * count, q * out_width : (q + 1) * out_width
            ]

    def elsewhere(c, q):
        return (c != my_clip) | (my_clip * ratio + q != me)

    @pl.loop(0, nc)
    def _(c):
        @pl.loop(0, ratio)
        def _(q):
            @pl.when(elsewhere(c, q))
            def _():
                block_copy(c, q).start()

            @pl.when(jnp.logical_not(elsewhere(c, q)))
            def _():
                landed_blocks[me] = blocks[c, q]

    @pl.loop(0, chunks)
    def _(k):
        @pl.when(k != me)
        def _():
            part_copy(k).wait_send()

        @pl.loop(0, n)
        def _(j):
            @pl.loop(0, pieces)
            def _(p):
                m = k * pieces + p

                @pl.when((j <= me) & (me < last))
                def _():
                    token_copy(0, m, j).wait_send()

                @pl.when((j >= me) & (me > 0))
                def _():
                    token_copy(1, m, j).wait_send()

            @pl.loop(0, tiles)
            def _(t):
                @pl.when(j > me)
                def _():
                    sum_copy(0, k, j, t).wait_send()

                @pl.when(j < me)
                def _():
                    sum_copy(1, k, j, t).wait_send()

    @pl.when(me < chunks)
    def _():
        @pl.loop(0, count)
        def _(c):
            @pl.when(c != me)
            def _():
                factor_copy(c).wait_send()

    @pl.when(me < count)
    def _():
        every_other(lambda c, z: sketch_copy(c, z).wait_send())

    other_clips(lambda c: partial_copy(c).wait_send())

    holds_own = (me >= my_clip * ratio) & (me < (my_clip + 1) * ratio)

    @pl.loop(0, n)
    def _(z):
        @pl.when((z != me) | jnp.logical_not(holds_own))
        def _():
            wait_for(landed_blocks.at[z], bl_recv.at[z])

    total = landed_blocks[0]
    for z in range(1, n):
        total += landed_blocks[z]
    out_ref[...] = total

    @pl.loop(0, nc)
    def _(c):
        @pl.loop(0, ratio)
        def _(q):
            @pl.when(elsewhere(c, q))
            def _():
                block_copy(c, q).wait_send()


CHUNKS = 4


def make_call(nc, n, rows, collective_id, args):
    clips, targets, lengths, gate, up, down, pin, pout, hessian, tests = args
    slots_all, width = clips.shape
    count = lengths.shape[0]
    hidden_part = gate.shape[1]
    proj = pin.shape[0]
    both = 2 * proj
    depth, columns = hessian.shape
    ratio = n // nc
    out_width = tests.shape[0] // ratio
    tile = 256 if hidden_part % 256 == 0 else hidden_part
    tile_w = 256 if width % 256 == 0 else width
    pieces = 2
    micro = CHUNKS * pieces
    ahead = 3
    vmem = pl.BlockSpec(memory_space=pltpu.VMEM)
    hbm = pl.BlockSpec(memory_space=pltpu.HBM)
    smem = pl.BlockSpec(memory_space=pltpu.SMEM)
    dma = pltpu.SemaphoreType.DMA
    tiles = width // tile_w
    return pl.pallas_call(
        functools.partial(scores_kernel, nc, n, CHUNKS, pieces, tile, ahead),
        out_shape=jax.ShapeDtypeStruct((count, out_width), F32),
        in_specs=[hbm, hbm, smem] + [hbm] * 7,
        out_specs=vmem,
        scratch_shapes=[
            pltpu.VMEM(clips.shape, BF16),
            pltpu.VMEM(targets.shape, BF16),
            pltpu.VMEM(pin.shape, BF16),
            pltpu.VMEM((both, hidden_part), BF16),
            pltpu.VMEM((both, width), BF16),
            pltpu.VMEM(gate.shape, BF16),
            pltpu.VMEM(up.shape, BF16),
            pltpu.VMEM(down.shape, BF16),
            pltpu.VMEM((micro, n, rows, width // pieces), BF16),
            pltpu.VMEM((CHUNKS, n + 1, tiles, rows, tile_w), BF16),
            pltpu.VMEM((CHUNKS, rows, hidden_part), BF16),
            pltpu.VMEM((CHUNKS, rows, both), F32),
            pltpu.VMEM((n, rows, both), F32),
            pltpu.VMEM((count, proj // 2, both), F32),
            pltpu.VMEM((CHUNKS, proj // 2, both), F32),
            pltpu.VMEM((nc, depth // both, both), F32),
            pltpu.VMEM((nc * count, depth // both, both), F32),
            pltpu.VMEM((nc * count, columns), F32),
            pltpu.VMEM((nc, nc * count, columns), F32),
            pltpu.VMEM((nc, ratio, count, out_width), F32),
            pltpu.VMEM((n, count, out_width), F32),
            dma((9,)),
            dma((2, micro, n)),
            dma((micro, n)),
            dma((CHUNKS, n, tiles)),
            dma((CHUNKS, n + 1, tiles)),
            dma((CHUNKS,)),
            dma((n,)),
            dma((count,)),
            dma((CHUNKS,)),
            dma((nc, n)),
            dma((nc * count,)),
            dma((nc,)),
            dma((nc,)),
            dma((nc, ratio)),
            dma((n,)),
        ],
        compiler_params=pltpu.CompilerParams(
            collective_id=collective_id,
            has_side_effects=True,
            vmem_limit_bytes=62 * 1024 * 1024,
        ),
        cost_estimate=pl.CostEstimate(
            flops=6 * CHUNKS * rows * hidden_part * width * n,
            bytes_accessed=2 * 3 * hidden_part * width * n,
            transcendentals=CHUNKS * rows * hidden_part,
        ),
        name=f"influence_{CHUNKS * rows}",
    )


def on_device(nc, n, *args):
    clips, targets = args[:2]
    count, clip_rows, width = clips.shape
    flat = (
        clips.reshape(count * clip_rows, width),
        targets.reshape(count * clip_rows, width),
        *args[2:],
    )
    return make_call(nc, n, count * clip_rows // CHUNKS, 0, flat)(*flat)


def solution(mesh):
    in_specs = (
        P(("parts", "clip"), None, "tensor"),
        P(("parts", "clip"), None, "tensor"),
        P(("parts", "clip")),
        P(None, "tensor"),
        P(None, "tensor"),
        P("tensor", None),
        P(None, "tensor"),
        P(),
        P("clip", "tensor"),
        P("clip", "tensor"),
    )
    out_specs = P(("parts", "clip"), "tensor")
    return jax.shard_map(
        functools.partial(on_device, mesh.shape["clip"], mesh.shape["tensor"]),
        mesh=mesh,
        in_specs=in_specs,
        out_specs=out_specs,
        check_vma=False,
    )
```

```python
import functools

import jax
import jax.numpy as jnp
from jax import lax
from jax.experimental import pallas as pl
from jax.experimental.pallas import tpu as pltpu
from jax.sharding import PartitionSpec as P

MESH = pl.DeviceIdType.MESH
BF16, F32 = jnp.bfloat16, jnp.float32


def wait_for(ref, sem):
    pltpu.make_async_copy(ref, ref, sem).wait()


def scores_kernel(
    nc,
    n,
    chunks,
    pieces,
    tile,
    ahead,
    clips_hbm,
    targets_hbm,
    lengths_ref,
    gate_hbm,
    up_hbm,
    down_hbm,
    pin_hbm,
    pout_hbm,
    hessian_hbm,
    tests_hbm,
    out_ref,
    clips_ref,
    targets_ref,
    source_ref,
    owner_ref,
    weight_ref,
    pin_raw,
    pin_ref,
    pout_ref,
    gate_ref,
    up_ref,
    down_ref,
    tok,
    slots,
    hid,
    joined,
    parts,
    factor,
    landed_factor,
    blocks_out,
    landed_sketch,
    partial,
    landed_partial,
    blocks,
    landed_blocks,
    load_sem,
    pair_send,
    pair_recv,
    ag_send,
    ag_recv,
    rs_send,
    rs_recv,
    own_send,
    own_recv,
    fa_send,
    fa_recv,
    sk_send,
    sk_recv,
    pp_send,
    pp_recv,
    bl_send,
    bl_recv,
):
    my_clip = lax.axis_index("clip")
    me = lax.axis_index("tensor")
    last = n - 1
    both_count = lengths_ref.shape[0]
    count = both_count // 2
    slots_all, width = clips_hbm.shape
    clip_rows = slots_all // count
    rows = hid.shape[1]
    core = my_clip % 2
    other = my_clip + 1 - 2 * core
    lanes = lengths_ref.shape[1]
    base = rows // count
    hidden_part = gate_ref.shape[1]
    proj = pin_hbm.shape[0]
    piece_w = width // pieces
    tile_w = slots.shape[-1]
    tiles = width // tile_w
    micro = chunks * pieces
    depth, columns = hessian_hbm.shape
    tests_part = tests_hbm.shape[0]
    out_width = out_ref.shape[1]
    ratio = n // nc
    per_block = depth // (2 * proj)

    load_clips = pltpu.make_async_copy(clips_hbm, clips_ref.at[core], load_sem.at[0])
    load_clips.start()
    loads = [
        pltpu.make_async_copy(pin_hbm, pin_raw, load_sem.at[1]),
        pltpu.make_async_copy(gate_hbm, gate_ref, load_sem.at[2]),
        pltpu.make_async_copy(up_hbm, up_ref, load_sem.at[3]),
        pltpu.make_async_copy(down_hbm, down_ref, load_sem.at[4]),
        pltpu.make_async_copy(
            pout_hbm.at[:, pl.ds(pl.multiple_of(me * width, width), width)],
            pout_ref.at[pl.ds(proj, proj)],
            load_sem.at[5],
        ),
    ]
    load_targets = pltpu.make_async_copy(targets_hbm, targets_ref.at[core], load_sem.at[6])
    hessian_ref = gate_ref.at[pl.ds(0, depth), pl.ds(0, columns)]
    tests_ref = up_ref.at[pl.ds(0, tests_part), pl.ds(0, columns)]
    load_hessian = pltpu.make_async_copy(hessian_hbm, hessian_ref, load_sem.at[7])
    load_tests = pltpu.make_async_copy(tests_hbm, tests_ref, load_sem.at[8])

    barrier = pltpu.get_barrier_semaphore()

    @pl.loop(0, nc)
    def _(c):
        @pl.loop(0, n)
        def _(z):
            @pl.when((c != my_clip) | (z != me))
            def _():
                pl.semaphore_signal(
                    barrier, inc=1, device_id={"clip": c, "tensor": z}, device_id_type=MESH
                )

    pin_ref[proj:, :] = jnp.zeros((proj, hidden_part), BF16)
    pout_ref[:proj, :] = jnp.zeros((proj, width), BF16)

    lengths = [jnp.broadcast_to(lengths_ref[i : i + 1, :], (rows, lanes)) for i in range(both_count)]
    ends = []
    for length in lengths:
        ends.append(length - base + (ends[-1] if ends else 0))
    row = lax.broadcasted_iota(jnp.int32, (rows, lanes), 0)

    def save_table(k, source, owner, valid):
        length = lengths[0]
        for i in range(1, both_count):
            length = jnp.where(owner == i, lengths[i], length)
        source_ref[k] = jnp.where(valid, source, -1)
        owner_ref[k] = jnp.where(valid, owner, -1)
        weight_ref[k] = jnp.where(valid, 1.0 / length.astype(F32), 0.0)

    def first_table():
        owner = jnp.zeros_like(row)
        for i in range(1, count):
            owner = owner + jnp.where(row >= i * base, 1, 0)
        source = owner * (clip_rows - base) + row
        save_table(0, source + core * slots_all, owner + core * count, row >= 0)

    def later_table(k):
        place = row + (core * (chunks - 1) + k - 1) * rows
        owner = jnp.zeros_like(row)
        source = place + base
        for i in range(both_count - 1):
            beyond = place >= ends[i]
            owner = owner + jnp.where(beyond, 1, 0)
            source = source + jnp.where(beyond, clip_rows + base - lengths[i], 0)
        save_table(k, source, owner, place < ends[-1])

    def pick(k, start, blocks_n):
        source = source_ref[k] - start
        lane = lax.broadcasted_iota(jnp.int32, (rows, lanes), 1)
        hits = [
            jnp.where(source == lane + b * lanes, 1.0, 0.0).astype(BF16) for b in range(blocks_n)
        ]
        return jnp.concatenate(hits, axis=1)

    def choose(chosen, ref, cols):
        return jnp.dot(
            chosen[:, :slots_all], ref[0, :, cols], preferred_element_type=F32
        ) + jnp.dot(chosen[:, slots_all:], ref[1, :, cols], preferred_element_type=F32)

    def pack_first():
        chosen = pick(0, core * slots_all, slots_all // lanes)
        for p in range(pieces):
            cols = slice(p * piece_w, (p + 1) * piece_w)
            tok[p, me] = jnp.dot(
                chosen, clips_ref[core, :, cols], preferred_element_type=F32
            ).astype(BF16)

    def pack_later(k):
        chosen = pick(k, 0, 2 * slots_all // lanes)
        for p in range(pieces):
            cols = slice(p * piece_w, (p + 1) * piece_w)
            tok[k * pieces + p, me] = choose(chosen, clips_ref, cols).astype(BF16)

    def pair_copy(i, ref):
        return pltpu.make_async_remote_copy(
            src_ref=ref.at[core],
            dst_ref=ref.at[core],
            send_sem=pair_send.at[i],
            recv_sem=pair_recv.at[i],
            device_id={"clip": other},
            device_id_type=MESH,
        )

    first_table()
    load_clips.wait()
    load_targets.start()
    for load in loads:
        load.start()
    pack_first()
    pl.semaphore_wait(barrier, nc * n - 1)

    def token_copy(side, m, j):
        target = me + 1 if side == 0 else me - 1
        return pltpu.make_async_remote_copy(
            src_ref=tok.at[m, j],
            dst_ref=tok.at[m, j],
            send_sem=ag_send.at[side, j],
            recv_sem=ag_recv.at[m, j],
            device_id={"tensor": target},
            device_id_type=MESH,
        )

    def sum_copy(side, k, d, t):
        if side == 0:
            target, slot = me + 1, d
        else:
            target = me - 1
            slot = jnp.where(d == me - 1, n, d)
        return pltpu.make_async_remote_copy(
            src_ref=slots.at[k, d, t],
            dst_ref=slots.at[k, slot, t],
            send_sem=rs_send.at[d],
            recv_sem=rs_recv.at[k, slot, t],
            device_id={"tensor": target},
            device_id_type=MESH,
        )

    def send_own(m):
        @pl.when(me < last)
        def _():
            token_copy(0, m, me).start()

        @pl.when(me > 0)
        def _():
            token_copy(1, m, me).start()

    def gather_step(m):
        @pl.loop(1, n)
        def _(h):
            q = m - h

            @pl.when((q >= 0) & (q < micro))
            def _():
                @pl.when(me - h >= 0)
                def _():
                    wait_for(tok.at[q, me - h], ag_recv.at[q, me - h])

                    @pl.when(me < last)
                    def _():
                        token_copy(0, q, me - h).start()

                @pl.when(me + h <= last)
                def _():
                    wait_for(tok.at[q, me + h], ag_recv.at[q, me + h])

                    @pl.when(me > 0)
                    def _():
                        token_copy(1, q, me + h).start()

        @pl.when(m + ahead < micro)
        def _():
            send_own(m + ahead)

    def partial_tile(k, d, t):
        start = pl.multiple_of(d * width + t * tile_w, tile_w)
        return jnp.dot(hid[k], down_ref[:, pl.ds(start, tile_w)], preferred_element_type=F32)

    def add_and_send(side, k, d):
        first = me == (0 if side == 0 else last)

        @pl.loop(0, tiles)
        def _(t):
            @pl.when(first)
            def _():
                slots[k, d, t] = partial_tile(k, d, t).astype(BF16)

            @pl.when(jnp.logical_not(first))
            def _():
                mine = partial_tile(k, d, t)
                wait_for(slots.at[k, d, t], rs_recv.at[k, d, t])
                slots[k, d, t] = (mine + slots[k, d, t].astype(F32)).astype(BF16)

            sum_copy(side, k, d, t).start()

    def hidden_tile(k, t):
        cols = pl.ds(pl.multiple_of(t * tile, tile), tile)
        gate_act = jnp.zeros((rows, tile), F32)
        up_act = jnp.zeros((rows, tile), F32)
        for j in range(n):
            for p in range(pieces):
                piece = tok[k * pieces + p, j]
                part = slice((j * pieces + p) * piece_w, (j * pieces + p + 1) * piece_w)
                gate_act += jnp.dot(piece, gate_ref[part, cols], preferred_element_type=F32)
                up_act += jnp.dot(piece, up_ref[part, cols], preferred_element_type=F32)
        silu = gate_act / (1.0 + jnp.exp(-gate_act))
        hid[k, :, cols] = (silu * up_act).astype(BF16)

    def join_left(k):
        joined[k] = lax.dot_general(
            hid[k], pin_ref[...], (((1,), (1,)), ((), ())), preferred_element_type=F32
        )

    def keeper(k):
        return (k + n // 2) % n

    kept = (me + n - n // 2) % n

    def part_copy(k):
        return pltpu.make_async_remote_copy(
            src_ref=joined.at[k],
            dst_ref=parts.at[me],
            send_sem=own_send.at[k],
            recv_sem=own_recv.at[me],
            device_id={"tensor": keeper(k)},
            device_id_type=MESH,
        )

    def finish(k):
        shape = (rows, tile_w)
        has_left = jnp.full(shape, jnp.where(me > 0, 1.0, 0.0), F32) > 0.5
        has_right = jnp.full(shape, jnp.where(me < last, 1.0, 0.0), F32) > 0.5
        weight = jnp.concatenate([weight_ref[k]] * (tile_w // lanes), axis=1)
        chosen = pick(k, 0, 2 * slots_all // lanes)

        @pl.loop(0, tiles)
        def _(t):
            cols = pl.ds(pl.multiple_of(t * tile_w, tile_w), tile_w)
            total = partial_tile(k, me, t)
            golden = choose(chosen, targets_ref, cols)

            @pl.when(me > 0)
            def _():
                wait_for(slots.at[k, me, t], rs_recv.at[k, me, t])

            @pl.when(me < last)
            def _():
                wait_for(slots.at[k, n, t], rs_recv.at[k, n, t])

            total += jnp.where(has_left, slots[k, me, t].astype(F32), 0.0)
            total += jnp.where(has_right, slots[k, n, t].astype(F32), 0.0)
            differ = jnp.clip(total - golden, -1.0, 1.0)
            grad = (differ * weight).astype(BF16)
            joined[k] += lax.dot_general(
                grad, pout_ref[:, cols], (((1,), (1,)), ((), ())), preferred_element_type=F32
            )

        @pl.when(me != keeper(k))
        def _():
            part_copy(k).start()

    @pl.loop(0, pieces)
    def _(m):
        send_own(m)

    pair_copy(0, clips_ref).start()

    @pl.loop(1, chunks)
    def _(k):
        later_table(k)

    load_targets.wait()
    pair_copy(1, targets_ref).start()
    wait_for(clips_ref.at[1 - core], pair_recv.at[0])

    @pl.loop(1, chunks)
    def _(k):
        pack_later(k)

    @pl.loop(pieces, ahead)
    def _(m):
        send_own(m)

    @pl.loop(0, pieces + last)
    def _(m):
        gather_step(m)

    loads[0].wait()
    order_row = lax.broadcasted_iota(jnp.int32, (proj, proj), 0)
    order_col = lax.broadcasted_iota(jnp.int32, (proj, proj), 1)
    half = proj // 2
    wanted = jnp.where(order_row < half, 2 * order_row, 2 * (order_row - half) + 1)
    shuffle = jnp.where(order_col == wanted, 1.0, 0.0).astype(BF16)
    pin_ref[:proj, :] = jnp.dot(shuffle, pin_raw[...], preferred_element_type=F32).astype(BF16)

    hidden_tiles = hidden_part // tile
    middle = hidden_tiles // 2

    @pl.loop(0, chunks + last)
    def _(k):
        upto = (k + 1) * pieces + last

        def more(i):
            @pl.when(upto + i < micro + last)
            def _():
                gather_step(upto + i)

        @pl.when(k == 0)
        def _():
            loads[1].wait()
            loads[2].wait()

        @pl.when(k < chunks)
        def _():
            @pl.loop(0, hidden_tiles)
            def _(t):
                hidden_tile(k, t)

            join_left(k)

        @pl.when(k == chunks - 1)
        def _():
            load_hessian.start()
            load_tests.start()

        @pl.when(k == 0)
        def _():
            for load in loads[3:]:
                load.wait()
            wait_for(targets_ref.at[1 - core], pair_recv.at[1])

        more(0)
        k_right = k - me

        @pl.when((k_right >= 0) & (k_right < chunks))
        def _():
            @pl.loop(0, last - me)
            def _(i):
                add_and_send(0, k_right, last - i)

        k_left = k - (last - me)

        @pl.when((k_left >= 0) & (k_left < chunks))
        def _():
            @pl.loop(0, me)
            def _(d):
                add_and_send(1, k_left, d)

        k_end = k - last

        @pl.when((k_end >= 0) & (k_end < chunks))
        def _():
            finish(k_end)

        for i in range(1, pieces):
            more(i)

    pair_start = my_clip - core

    def factor_copy(h, c):
        return pltpu.make_async_remote_copy(
            src_ref=factor.at[h, c],
            dst_ref=landed_factor.at[core, kept],
            send_sem=fa_send.at[h, c],
            recv_sem=fa_recv.at[core, kept],
            device_id={"clip": pair_start + h, "tensor": c},
            device_id_type=MESH,
        )

    def other_factors(act):
        @pl.loop(0, 2)
        def _(h):
            @pl.loop(0, count)
            def _(c):
                @pl.when((h != core) | (c != me))
                def _():
                    act(h, c)

    @pl.when(kept < chunks)
    def _():
        parts[me] = joined[kept]

        @pl.loop(0, n)
        def _(j):
            @pl.when(j != me)
            def _():
                wait_for(parts.at[j], own_recv.at[j])

        total = parts[0]
        for j in range(1, n):
            total += parts[j]
        lane = lax.broadcasted_iota(jnp.int32, (rows, 2 * proj), 1)
        right = jnp.where(lane < proj, pltpu.roll(total, proj, 1), total)
        owner = owner_ref[kept]
        product = jnp.dot(
            total.T[:proj],
            jnp.concatenate(
                [jnp.where(owner == i, right, 0.0) for i in range(both_count)], axis=1
            ),
            precision=lax.Precision.HIGHEST,
            preferred_element_type=F32,
        )
        low = lax.broadcasted_iota(jnp.int32, (half, 2 * proj), 1) < proj
        for i in range(both_count):
            block = product[:, i * 2 * proj : (i + 1) * 2 * proj]
            factor[i // count, i % count] = jnp.where(low, block[:half], block[half:])
        other_factors(lambda h, c: factor_copy(h, c).start())

    def sketch_copy(c, z):
        return pltpu.make_async_remote_copy(
            src_ref=blocks_out.at[c],
            dst_ref=landed_sketch.at[my_clip * count + me],
            send_sem=sk_send.at[c, z],
            recv_sem=sk_recv.at[my_clip * count + me],
            device_id={"clip": c, "tensor": z},
            device_id_type=MESH,
        )

    def every_other(act):
        @pl.loop(0, nc)
        def _(c):
            @pl.loop(0, n)
            def _(z):
                @pl.when((c != my_clip) | (z != me))
                def _():
                    act(c, z)

    @pl.when(me < count)
    def _():
        @pl.when(kept < chunks)
        def _():
            landed_factor[core, kept] = factor[core, me]

        @pl.loop(0, 2)
        def _(h):
            @pl.loop(0, chunks)
            def _(k):
                @pl.when((h != core) | (k != kept))
                def _():
                    wait_for(landed_factor.at[h, k], fa_recv.at[h, k])

        total = landed_factor[0, 0]
        for k in range(1, 2 * chunks):
            total += landed_factor[k // chunks, k % chunks]
        total = total.astype(BF16).astype(F32)
        for c in range(nc):
            blocks_out[c] = total[c * per_block : (c + 1) * per_block]
        every_other(lambda c, z: sketch_copy(c, z).start())
        landed_sketch[my_clip * count + me] = blocks_out[my_clip]

    @pl.loop(0, nc)
    def _(c):
        @pl.loop(0, count)
        def _(z):
            @pl.when((c != my_clip) | (z != me))
            def _():
                wait_for(landed_sketch.at[c * count + z], sk_recv.at[c * count + z])

    def partial_copy(c):
        return pltpu.make_async_remote_copy(
            src_ref=partial,
            dst_ref=landed_partial.at[my_clip],
            send_sem=pp_send.at[c],
            recv_sem=pp_recv.at[my_clip],
            device_id={"clip": c, "tensor": me},
            device_id_type=MESH,
        )

    def block_copy(c, q):
        return pltpu.make_async_remote_copy(
            src_ref=blocks.at[c, q],
            dst_ref=landed_blocks.at[me],
            send_sem=bl_send.at[c, q],
            recv_sem=bl_recv.at[me],
            device_id={"clip": c, "tensor": my_clip * ratio + q},
            device_id_type=MESH,
        )

    def other_clips(act):
        @pl.loop(0, nc)
        def _(c):
            @pl.when(c != my_clip)
            def _():
                act(c)

    load_hessian.wait()
    stacked = jnp.concatenate([landed_sketch[:, r, :] for r in range(per_block)], axis=1)
    partial[...] = jnp.dot(
        stacked.astype(BF16), hessian_ref[...], preferred_element_type=F32
    )
    other_clips(lambda c: partial_copy(c).start())
    landed_partial[my_clip] = partial[...]
    load_tests.wait()
    other_clips(lambda c: wait_for(landed_partial.at[c], pp_recv.at[c]))
    precond = landed_partial[0]
    for c in range(1, nc):
        precond += landed_partial[c]
    scores = lax.dot_general(
        precond.astype(BF16),
        tests_ref[...],
        (((1,), (1,)), ((), ())),
        preferred_element_type=F32,
    )
    for c in range(nc):
        for q in range(ratio):
            blocks[c, q] = scores[
                c * count : (c + 1) * count, q * out_width : (q + 1) * out_width
            ]

    def elsewhere(c, q):
        return (c != my_clip) | (my_clip * ratio + q != me)

    @pl.loop(0, nc)
    def _(c):
        @pl.loop(0, ratio)
        def _(q):
            @pl.when(elsewhere(c, q))
            def _():
                block_copy(c, q).start()

            @pl.when(jnp.logical_not(elsewhere(c, q)))
            def _():
                landed_blocks[me] = blocks[c, q]

    pair_copy(0, clips_ref).wait_send()
    pair_copy(1, targets_ref).wait_send()

    @pl.loop(0, chunks)
    def _(k):
        @pl.when(me != keeper(k))
        def _():
            part_copy(k).wait_send()

    @pl.loop(0, n)
    def _(j):
        @pl.when((j <= me) & (me < last))
        def _():
            wait_for(tok.at[:, j], ag_send.at[0, j])

        @pl.when((j >= me) & (me > 0))
        def _():
            wait_for(tok.at[:, j], ag_send.at[1, j])

        @pl.when(j != me)
        def _():
            wait_for(slots.at[:, j], rs_send.at[j])

    @pl.when(kept < chunks)
    def _():
        other_factors(lambda h, c: factor_copy(h, c).wait_send())

    @pl.when(me < count)
    def _():
        every_other(lambda c, z: sketch_copy(c, z).wait_send())

    other_clips(lambda c: partial_copy(c).wait_send())

    holds_own = (me >= my_clip * ratio) & (me < (my_clip + 1) * ratio)

    @pl.loop(0, n)
    def _(z):
        @pl.when((z != me) | jnp.logical_not(holds_own))
        def _():
            wait_for(landed_blocks.at[z], bl_recv.at[z])

    total = landed_blocks[0]
    for z in range(1, n):
        total += landed_blocks[z]
    out_ref[...] = total

    @pl.loop(0, nc)
    def _(c):
        @pl.loop(0, ratio)
        def _(q):
            @pl.when(elsewhere(c, q))
            def _():
                block_copy(c, q).wait_send()


def agree_kernel(
    capacities, parts_n, nc, lengths_ref, index_ref, pair_ref, landed, send_sem, recv_sem
):
    my_clip = lax.axis_index("clip")
    mine = lax.axis_index("parts") * nc + my_clip
    count = lengths_ref.shape[0]
    groups = parts_n * nc

    def others(act):
        @pl.loop(0, parts_n)
        def _(y):
            @pl.loop(0, nc)
            def _(c):
                @pl.when(y * nc + c != mine)
                def _():
                    act(y, c)

    barrier = pltpu.get_barrier_semaphore()
    others(
        lambda y, c: pl.semaphore_signal(
            barrier, inc=1, device_id={"parts": y, "clip": c}, device_id_type=MESH
        )
    )
    sublane = lax.broadcasted_iota(jnp.int32, landed.shape[1:], 0)
    tile = jnp.zeros(landed.shape[1:], jnp.int32)
    for i in range(count):
        tile = jnp.where(sublane == i, lengths_ref[i], tile)
    landed[mine] = tile
    pl.semaphore_wait(barrier, groups - 1)

    def lengths_copy(y, c):
        return pltpu.make_async_remote_copy(
            src_ref=landed.at[mine],
            dst_ref=landed.at[mine],
            send_sem=send_sem.at[y * nc + c],
            recv_sem=recv_sem.at[mine],
            device_id={"parts": y, "clip": c},
            device_id_type=MESH,
        )

    others(lambda y, c: lengths_copy(y, c).start())
    others(
        lambda y, c: wait_for(landed.at[y * nc + c], recv_sem.at[y * nc + c])
    )
    most = jnp.zeros((1, landed.shape[2]), jnp.int32)
    for g in range(0, groups, 2):
        pair = landed[g] + landed[g + 1]
        total = pair[0:1]
        for i in range(1, count):
            total = total + pair[i : i + 1]
        most = jnp.maximum(most, total)
    index = jnp.zeros_like(most)
    for capacity in capacities[:-1]:
        index = index + jnp.where(most > 2 * capacity, 1, 0)
    index_ref[0] = jnp.max(index)
    start = mine - my_clip % 2
    pair_ref[0:count] = landed[start, 0:count]
    pair_ref[count:] = landed[start + 1, 0:count]
    others(lambda y, c: lengths_copy(y, c).wait_send())


def agree(capacities, parts_n, nc, lengths):
    count = lengths.shape[0]
    groups = parts_n * nc
    return pl.pallas_call(
        functools.partial(agree_kernel, capacities, parts_n, nc),
        out_shape=(
            jax.ShapeDtypeStruct((1,), jnp.int32),
            jax.ShapeDtypeStruct((2 * count, 128), jnp.int32),
        ),
        in_specs=[pl.BlockSpec(memory_space=pltpu.SMEM)],
        out_specs=(
            pl.BlockSpec(memory_space=pltpu.SMEM),
            pl.BlockSpec(memory_space=pltpu.VMEM),
        ),
        scratch_shapes=[
            pltpu.VMEM((groups, 8, 128), jnp.int32),
            pltpu.SemaphoreType.DMA((groups,)),
            pltpu.SemaphoreType.DMA((groups,)),
        ],
        compiler_params=pltpu.CompilerParams(collective_id=0, has_side_effects=True),
        name="agree",
    )(lengths)


CHUNKS = 4


def make_call(nc, n, rows, collective_id, args):
    clips, targets, lengths, gate, up, down, pin, pout, hessian, tests = args
    slots_all, width = clips.shape
    both_count = lengths.shape[0]
    count = both_count // 2
    hidden_part = gate.shape[1]
    proj = pin.shape[0]
    both = 2 * proj
    depth, columns = hessian.shape
    ratio = n // nc
    out_width = tests.shape[0] // ratio
    tile = 256 if hidden_part % 256 == 0 else hidden_part
    tile_w = 256 if width % 256 == 0 else width
    pieces = 2
    micro = CHUNKS * pieces
    ahead = 3
    vmem = pl.BlockSpec(memory_space=pltpu.VMEM)
    hbm = pl.BlockSpec(memory_space=pltpu.HBM)
    dma = pltpu.SemaphoreType.DMA
    tiles = width // tile_w
    return pl.pallas_call(
        functools.partial(scores_kernel, nc, n, CHUNKS, pieces, tile, ahead),
        out_shape=jax.ShapeDtypeStruct((count, out_width), F32),
        in_specs=[hbm, hbm, vmem] + [hbm] * 7,
        out_specs=vmem,
        scratch_shapes=[
            pltpu.VMEM((2, *clips.shape), BF16),
            pltpu.VMEM((2, *targets.shape), BF16),
            pltpu.VMEM((CHUNKS, rows, 128), jnp.int32),
            pltpu.VMEM((CHUNKS, rows, 128), jnp.int32),
            pltpu.VMEM((CHUNKS, rows, 128), F32),
            pltpu.VMEM(pin.shape, BF16),
            pltpu.VMEM((both, hidden_part), BF16),
            pltpu.VMEM((both, width), BF16),
            pltpu.VMEM(gate.shape, BF16),
            pltpu.VMEM(up.shape, BF16),
            pltpu.VMEM(down.shape, BF16),
            pltpu.VMEM((micro, n, rows, width // pieces), BF16),
            pltpu.VMEM((CHUNKS, n + 1, tiles, rows, tile_w), BF16),
            pltpu.VMEM((CHUNKS, rows, hidden_part), BF16),
            pltpu.VMEM((CHUNKS, rows, both), F32),
            pltpu.VMEM((n, rows, both), F32),
            pltpu.VMEM((2, count, proj // 2, both), F32),
            pltpu.VMEM((2, CHUNKS, proj // 2, both), F32),
            pltpu.VMEM((nc, depth // both, both), F32),
            pltpu.VMEM((nc * count, depth // both, both), F32),
            pltpu.VMEM((nc * count, columns), F32),
            pltpu.VMEM((nc, nc * count, columns), F32),
            pltpu.VMEM((nc, ratio, count, out_width), F32),
            pltpu.VMEM((n, count, out_width), F32),
            dma((9,)),
            dma((2,)),
            dma((2,)),
            dma((2, n)),
            dma((micro, n)),
            dma((n,)),
            dma((CHUNKS, n + 1, tiles)),
            dma((CHUNKS,)),
            dma((n,)),
            dma((2, count)),
            dma((2, CHUNKS)),
            dma((nc, n)),
            dma((nc * count,)),
            dma((nc,)),
            dma((nc,)),
            dma((nc, ratio)),
            dma((n,)),
        ],
        compiler_params=pltpu.CompilerParams(
            collective_id=collective_id,
            has_side_effects=True,
            vmem_limit_bytes=62 * 1024 * 1024,
        ),
        cost_estimate=pl.CostEstimate(
            flops=6 * CHUNKS * rows * hidden_part * width * n,
            bytes_accessed=2 * 3 * hidden_part * width * n,
            transcendentals=CHUNKS * rows * hidden_part,
        ),
        name=f"influence_{CHUNKS * rows}",
    )


def on_device(parts_n, nc, n, *args):
    clips, targets, lengths = args[:3]
    count, clip_rows, width = clips.shape
    slots_all = count * clip_rows
    step = slots_all // 8
    capacities = [step * i for i in (6, 7, 8)]
    index, pair_lengths = agree(capacities, parts_n, nc, lengths)
    flat = (
        clips.reshape(slots_all, width),
        targets.reshape(slots_all, width),
        pair_lengths,
        *args[3:],
    )
    calls = [
        make_call(nc, n, capacity // CHUNKS, 1 + i, flat)
        for i, capacity in enumerate(capacities)
    ]
    return lax.switch(index[0], calls, *flat)


def solution(mesh):
    in_specs = (
        P(("parts", "clip"), None, "tensor"),
        P(("parts", "clip"), None, "tensor"),
        P(("parts", "clip")),
        P(None, "tensor"),
        P(None, "tensor"),
        P("tensor", None),
        P(None, "tensor"),
        P(),
        P("clip", "tensor"),
        P("clip", "tensor"),
    )
    out_specs = P(("parts", "clip"), "tensor")
    return jax.shard_map(
        functools.partial(
            on_device, mesh.shape["parts"], mesh.shape["clip"], mesh.shape["tensor"]
        ),
        mesh=mesh,
        in_specs=in_specs,
        out_specs=out_specs,
        check_vma=False,
    )
```

```python
import functools

import jax
import jax.numpy as jnp
from jax import lax
from jax.experimental import pallas as pl
from jax.experimental.pallas import tpu as pltpu
from jax.sharding import PartitionSpec as P

MESH = pl.DeviceIdType.MESH
BF16, F32 = jnp.bfloat16, jnp.float32


def wait_for(ref, sem):
    pltpu.make_async_copy(ref, ref, sem).wait()


def scores_kernel(
    nc,
    n,
    sizes,
    rows,
    tile,
    ahead,
    clips_hbm,
    targets_hbm,
    lengths_ref,
    gate_hbm,
    up_hbm,
    down_hbm,
    pin_hbm,
    pout_hbm,
    hessian_hbm,
    tests_hbm,
    out_ref,
    clips_ref,
    targets_ref,
    source_ref,
    owner_ref,
    weight_ref,
    pin_raw,
    pin_ref,
    pout_ref,
    gate_ref,
    up_ref,
    down_ref,
    tok,
    slots,
    hid,
    joined,
    parts,
    product,
    factor,
    landed_factor,
    blocks_out,
    landed_sketch,
    partial,
    landed_partial,
    blocks,
    landed_blocks,
    load_sem,
    pair_send,
    pair_recv,
    ag_send,
    ag_recv,
    rs_send,
    rs_recv,
    own_send,
    own_recv,
    fa_send,
    fa_recv,
    sk_send,
    sk_recv,
    pp_send,
    pp_recv,
    bl_send,
    bl_recv,
):
    my_clip = lax.axis_index("clip")
    me = lax.axis_index("tensor")
    last = n - 1
    both_count = lengths_ref.shape[0]
    count = both_count // 2
    slots_all, width = clips_hbm.shape
    clip_rows = slots_all // count
    core = my_clip % 2
    other = my_clip + 1 - 2 * core
    lanes = lengths_ref.shape[1]
    base = sizes[0] * rows // count
    hidden_part = gate_ref.shape[1]
    proj = pin_hbm.shape[0]
    steps = len(sizes)
    cuts = [part for size in sizes for part in (size - size // 2, size // 2)]
    pieces = len(cuts)
    units = sum(sizes)
    tile_w = slots.shape[-1]
    tiles = width // tile_w

    def span(first, size):
        return pl.ds(pl.multiple_of(first * rows, rows), size * rows)

    def begin(k):
        return sum(jnp.where(k > i, size, 0) for i, size in enumerate(sizes))

    def piece_begin(m):
        return sum(jnp.where(m > i, size, 0) for i, size in enumerate(cuts))

    def by_length(lengths_of, start_of, k, act):
        for size in sorted(set(lengths_of)):
            same = [k == i for i, other_size in enumerate(lengths_of) if other_size == size]

            @pl.when(functools.reduce(jnp.logical_or, same))
            def _(size=size):
                act(k, start_of(k), size)

    by_size = functools.partial(by_length, sizes, begin)
    by_piece = functools.partial(by_length, cuts, piece_begin)
    depth, columns = hessian_hbm.shape
    tests_part = tests_hbm.shape[0]
    out_width = out_ref.shape[1]
    ratio = n // nc
    per_block = depth // (2 * proj)

    load_clips = pltpu.make_async_copy(clips_hbm, clips_ref.at[core], load_sem.at[0])
    load_clips.start()
    loads = [
        pltpu.make_async_copy(pin_hbm, pin_raw, load_sem.at[1]),
        pltpu.make_async_copy(gate_hbm, gate_ref, load_sem.at[2]),
        pltpu.make_async_copy(up_hbm, up_ref, load_sem.at[3]),
        pltpu.make_async_copy(down_hbm, down_ref, load_sem.at[4]),
        pltpu.make_async_copy(
            pout_hbm.at[:, pl.ds(pl.multiple_of(me * width, width), width)],
            pout_ref.at[pl.ds(proj, proj)],
            load_sem.at[5],
        ),
    ]
    load_targets = pltpu.make_async_copy(targets_hbm, targets_ref.at[core], load_sem.at[6])
    hessian_ref = gate_ref.at[pl.ds(0, depth), pl.ds(0, columns)]
    tests_ref = up_ref.at[pl.ds(0, tests_part), pl.ds(0, columns)]
    load_hessian = pltpu.make_async_copy(hessian_hbm, hessian_ref, load_sem.at[7])
    load_tests = pltpu.make_async_copy(tests_hbm, tests_ref, load_sem.at[8])

    barrier = pltpu.get_barrier_semaphore()

    @pl.loop(0, nc)
    def _(c):
        @pl.loop(0, n)
        def _(z):
            @pl.when((c != my_clip) | (z != me))
            def _():
                pl.semaphore_signal(
                    barrier, inc=1, device_id={"clip": c, "tensor": z}, device_id_type=MESH
                )

    pin_ref[proj:, :] = jnp.zeros((proj, hidden_part), BF16)
    pout_ref[:proj, :] = jnp.zeros((proj, width), BF16)

    lengths = [jnp.broadcast_to(lengths_ref[i : i + 1, :], (rows, lanes)) for i in range(both_count)]
    ends = []
    for length in lengths:
        ends.append(length - base + (ends[-1] if ends else 0))
    row = lax.broadcasted_iota(jnp.int32, (rows, lanes), 0)

    def save_table(m, source, owner, valid):
        length = lengths[0]
        for i in range(1, both_count):
            length = jnp.where(owner == i, lengths[i], length)
        where = span(m, 1)
        source_ref[where] = jnp.where(valid, source, -1)
        owner_ref[where] = jnp.where(valid, owner, -1)
        weight_ref[where] = jnp.where(valid, 1.0 / length.astype(F32), 0.0)

    def first_table(m):
        place = row + m * rows
        owner = jnp.zeros_like(row)
        for i in range(1, count):
            owner = owner + jnp.where(place >= i * base, 1, 0)
        source = owner * (clip_rows - base) + place
        save_table(m, source + core * slots_all, owner + core * count, row >= 0)

    def later_table(m):
        place = row + (core * (units - sizes[0]) + m - sizes[0]) * rows
        owner = jnp.zeros_like(row)
        source = place + base
        for i in range(both_count - 1):
            beyond = place >= ends[i]
            owner = owner + jnp.where(beyond, 1, 0)
            source = source + jnp.where(beyond, clip_rows + base - lengths[i], 0)
        save_table(m, source, owner, place < ends[-1])

    def pick(first, size, start, blocks_n):
        source = source_ref[span(first, size)] - start
        lane = lax.broadcasted_iota(jnp.int32, source.shape, 1)
        hits = [
            jnp.where(source == lane + b * lanes, 1.0, 0.0).astype(BF16) for b in range(blocks_n)
        ]
        return jnp.concatenate(hits, axis=1)

    def choose(chosen, ref, cols):
        return jnp.dot(
            chosen[:, :slots_all], ref[0, :, cols], preferred_element_type=F32
        ) + jnp.dot(chosen[:, slots_all:], ref[1, :, cols], preferred_element_type=F32)

    def pack_first():
        chosen = pick(0, sizes[0], core * slots_all, slots_all // lanes)

        @pl.loop(0, tiles)
        def _(t):
            cols = pl.ds(pl.multiple_of(t * tile_w, tile_w), tile_w)
            tok[me, span(0, sizes[0]), cols] = jnp.dot(
                chosen, clips_ref[core, :, cols], preferred_element_type=F32
            ).astype(BF16)

    def pack_later(k, first, size):
        chosen = pick(first, size, 0, 2 * slots_all // lanes)

        @pl.loop(0, tiles)
        def _(t):
            cols = pl.ds(pl.multiple_of(t * tile_w, tile_w), tile_w)
            tok[me, span(first, size), cols] = choose(chosen, clips_ref, cols).astype(BF16)

    def pair_copy(i, ref):
        return pltpu.make_async_remote_copy(
            src_ref=ref.at[core],
            dst_ref=ref.at[core],
            send_sem=pair_send.at[i],
            recv_sem=pair_recv.at[i],
            device_id={"clip": other},
            device_id_type=MESH,
        )


    @pl.loop(0, sizes[0])
    def _(m):
        first_table(m)

    load_clips.wait()
    load_targets.start()
    for load in loads:
        load.start()
    pack_first()
    pl.semaphore_wait(barrier, nc * n - 1)

    def token_copy(side, m, first, size, j):
        target = me + 1 if side == 0 else me - 1
        return pltpu.make_async_remote_copy(
            src_ref=tok.at[j, span(first, size)],
            dst_ref=tok.at[j, span(first, size)],
            send_sem=ag_send.at[side, j],
            recv_sem=ag_recv.at[m, j],
            device_id={"tensor": target},
            device_id_type=MESH,
        )

    def sum_copy(side, k, first, size, d, t):
        if side == 0:
            target, slot = me + 1, d
        else:
            target = me - 1
            slot = jnp.where(d == me - 1, n, d)
        return pltpu.make_async_remote_copy(
            src_ref=slots.at[d, t, span(first, size)],
            dst_ref=slots.at[slot, t, span(first, size)],
            send_sem=rs_send.at[d],
            recv_sem=rs_recv.at[k, slot, t],
            device_id={"tensor": target},
            device_id_type=MESH,
        )

    def send_own(m):
        def act(m, first, size):
            @pl.when(me < last)
            def _():
                token_copy(0, m, first, size, me).start()

            @pl.when(me > 0)
            def _():
                token_copy(1, m, first, size, me).start()

        by_piece(m, act)

    def gather_step(m):
        @pl.loop(1, n)
        def _(h):
            def act(q, first, size):
                @pl.when(me - h >= 0)
                def _():
                    wait_for(tok.at[me - h, span(first, size)], ag_recv.at[q, me - h])

                    @pl.when(me < last)
                    def _():
                        token_copy(0, q, first, size, me - h).start()

                @pl.when(me + h <= last)
                def _():
                    wait_for(tok.at[me + h, span(first, size)], ag_recv.at[q, me + h])

                    @pl.when(me > 0)
                    def _():
                        token_copy(1, q, first, size, me + h).start()

            by_piece(m - h, act)

        @pl.when(m + ahead < pieces)
        def _():
            send_own(m + ahead)

    def partial_tile(first, size, d, t):
        start = pl.multiple_of(d * width + t * tile_w, tile_w)
        return jnp.dot(
            hid[span(first, size)], down_ref[:, pl.ds(start, tile_w)], preferred_element_type=F32
        )

    def add_and_send(side, k, first, size, d):
        leading = me == (0 if side == 0 else last)

        @pl.loop(0, tiles)
        def _(t):
            where = span(first, size)

            @pl.when(leading)
            def _():
                slots[d, t, where] = partial_tile(first, size, d, t).astype(BF16)

            @pl.when(jnp.logical_not(leading))
            def _():
                mine = partial_tile(first, size, d, t)
                wait_for(slots.at[d, t, where], rs_recv.at[k, d, t])
                slots[d, t, where] = (mine + slots[d, t, where].astype(F32)).astype(BF16)

            sum_copy(side, k, first, size, d, t).start()

    def hidden_tile(first, size, t):
        cols = pl.ds(pl.multiple_of(t * tile, tile), tile)
        gate_act = jnp.zeros((size * rows, tile), F32)
        up_act = jnp.zeros((size * rows, tile), F32)
        for j in range(n):
            piece = tok[j, span(first, size)]
            part = slice(j * width, (j + 1) * width)
            gate_act += jnp.dot(piece, gate_ref[part, cols], preferred_element_type=F32)
            up_act += jnp.dot(piece, up_ref[part, cols], preferred_element_type=F32)
        silu = gate_act / (1.0 + jnp.exp(-gate_act))
        hid[span(first, size), cols] = (silu * up_act).astype(BF16)

    def join_left(first, size):
        joined[span(first, size)] = lax.dot_general(
            hid[span(first, size)],
            pin_ref[...],
            (((1,), (1,)), ((), ())),
            preferred_element_type=F32,
        )

    shift = (n + n // 2 - steps) % n

    def keeper(k):
        return (k + shift) % n

    kept = (me + n - shift) % n

    def part_copy(k, first, size):
        return pltpu.make_async_remote_copy(
            src_ref=joined.at[span(first, size)],
            dst_ref=parts.at[k // n, me, pl.ds(0, size * rows)],
            send_sem=own_send.at[k],
            recv_sem=own_recv.at[k // n, me],
            device_id={"tensor": keeper(k)},
            device_id_type=MESH,
        )

    def finish(k, first, size):
        shape = (size * rows, tile_w)
        has_left = jnp.full(shape, jnp.where(me > 0, 1.0, 0.0), F32) > 0.5
        has_right = jnp.full(shape, jnp.where(me < last, 1.0, 0.0), F32) > 0.5
        where = span(first, size)
        weight = jnp.concatenate([weight_ref[where]] * (tile_w // lanes), axis=1)
        chosen = pick(first, size, 0, 2 * slots_all // lanes)

        @pl.loop(0, tiles)
        def _(t):
            cols = pl.ds(pl.multiple_of(t * tile_w, tile_w), tile_w)
            total = partial_tile(first, size, me, t)
            golden = choose(chosen, targets_ref, cols)

            @pl.when(me > 0)
            def _():
                wait_for(slots.at[me, t, where], rs_recv.at[k, me, t])

            @pl.when(me < last)
            def _():
                wait_for(slots.at[n, t, where], rs_recv.at[k, n, t])

            total += jnp.where(has_left, slots[me, t, where].astype(F32), 0.0)
            total += jnp.where(has_right, slots[n, t, where].astype(F32), 0.0)
            differ = jnp.clip(total - golden, -1.0, 1.0)
            grad = (differ * weight).astype(BF16)
            joined[where] += lax.dot_general(
                grad, pout_ref[:, cols], (((1,), (1,)), ((), ())), preferred_element_type=F32
            )

        @pl.when(me != keeper(k))
        def _():
            part_copy(k, first, size).start()

    @pl.loop(0, 2)
    def _(m):
        send_own(m)

    pair_copy(0, clips_ref).start()

    @pl.loop(sizes[0], units)
    def _(m):
        later_table(m)

    load_targets.wait()
    pair_copy(1, targets_ref).start()
    wait_for(clips_ref.at[1 - core], pair_recv.at[0])

    @pl.loop(1, steps)
    def _(k):
        by_size(k, pack_later)

    @pl.loop(2, ahead)
    def _(m):
        send_own(m)

    @pl.loop(0, 2 + last)
    def _(m):
        gather_step(m)

    loads[0].wait()
    order_row = lax.broadcasted_iota(jnp.int32, (proj, proj), 0)
    order_col = lax.broadcasted_iota(jnp.int32, (proj, proj), 1)
    half = proj // 2
    wanted = jnp.where(order_row < half, 2 * order_row, 2 * (order_row - half) + 1)
    shuffle = jnp.where(order_col == wanted, 1.0, 0.0).astype(BF16)
    pin_ref[:proj, :] = jnp.dot(shuffle, pin_raw[...], preferred_element_type=F32).astype(BF16)

    hidden_tiles = hidden_part // tile

    @pl.loop(0, steps + last)
    def _(k):
        upto = 2 * (k + 1) + last

        def more(i):
            @pl.when(upto + i < pieces + last)
            def _():
                gather_step(upto + i)

        @pl.when(k == 0)
        def _():
            loads[1].wait()
            loads[2].wait()

        def make_hidden(k, first, size):
            @pl.loop(0, hidden_tiles)
            def _(t):
                hidden_tile(first, size, t)

            join_left(first, size)

        by_size(k, make_hidden)

        @pl.when(k == steps - 1)
        def _():
            load_hessian.start()
            load_tests.start()

        @pl.when(k == 0)
        def _():
            for load in loads[3:]:
                load.wait()
            wait_for(targets_ref.at[1 - core], pair_recv.at[1])

        more(0)

        def send_right(k, first, size):
            @pl.loop(0, last - me)
            def _(i):
                add_and_send(0, k, first, size, last - i)

        by_size(k - me, send_right)

        def send_left(k, first, size):
            @pl.loop(0, me)
            def _(d):
                add_and_send(1, k, first, size, d)

        by_size(k - (last - me), send_left)
        by_size(k - last, finish)
        more(1)

    pair_start = my_clip - core

    def factor_copy(h, c):
        return pltpu.make_async_remote_copy(
            src_ref=factor.at[h, c],
            dst_ref=landed_factor.at[core, me],
            send_sem=fa_send.at[h, c],
            recv_sem=fa_recv.at[core, me],
            device_id={"clip": pair_start + h, "tensor": c},
            device_id_type=MESH,
        )

    def other_factors(act):
        @pl.loop(0, 2)
        def _(h):
            @pl.loop(0, count)
            def _(c):
                @pl.when((h != core) | (c != me))
                def _():
                    act(h, c)

    def add_product(k, first, size):
        held = pl.ds(0, size * rows)
        total = joined[span(first, size)]

        @pl.loop(0, n)
        def _(j):
            @pl.when(j != me)
            def _():
                wait_for(parts.at[k // n, j, held], own_recv.at[k // n, j])

        parts[k // n, me, held] = total
        total = parts[k // n, 0, held]
        for j in range(1, n):
            total += parts[k // n, j, held]
        lane = lax.broadcasted_iota(jnp.int32, total.shape, 1)
        right = jnp.where(lane < proj, pltpu.roll(total, proj, 1), total)
        owner = owner_ref[span(first, size)]
        product[...] += jnp.dot(
            total.T[:proj],
            jnp.concatenate(
                [jnp.where(owner == i, right, 0.0) for i in range(both_count)], axis=1
            ),
            precision=lax.Precision.HIGHEST,
            preferred_element_type=F32,
        )

    def is_keeper(z):
        return (z + n - shift) % n < steps

    @pl.when(is_keeper(me))
    def _():
        product[...] = jnp.zeros_like(product)
        for i in range(parts.shape[0]):
            by_size(kept + i * n, add_product)
        low = lax.broadcasted_iota(jnp.int32, (half, 2 * proj), 1) < proj
        for i in range(both_count):
            cols = slice(i * 2 * proj, (i + 1) * 2 * proj)
            factor[i // count, i % count] = jnp.where(
                low, product[:half, cols], product[half:, cols]
            )
        other_factors(lambda h, c: factor_copy(h, c).start())

    def sketch_copy(c, z):
        return pltpu.make_async_remote_copy(
            src_ref=blocks_out.at[c],
            dst_ref=landed_sketch.at[my_clip * count + me],
            send_sem=sk_send.at[c, z],
            recv_sem=sk_recv.at[my_clip * count + me],
            device_id={"clip": c, "tensor": z},
            device_id_type=MESH,
        )

    def every_other(act):
        @pl.loop(0, nc)
        def _(c):
            @pl.loop(0, n)
            def _(z):
                @pl.when((c != my_clip) | (z != me))
                def _():
                    act(c, z)

    @pl.when(me < count)
    def _():
        @pl.when(is_keeper(me))
        def _():
            landed_factor[core, me] = factor[core, me]

        if steps < n:
            @pl.loop(0, n)
            def _(z):
                @pl.when(jnp.logical_not(is_keeper(z)))
                def _():
                    landed_factor[0, z] = jnp.zeros_like(landed_factor[0, z])
                    landed_factor[1, z] = jnp.zeros_like(landed_factor[1, z])

        @pl.loop(0, 2)
        def _(h):
            @pl.loop(0, n)
            def _(z):
                @pl.when(((h != core) | (z != me)) & is_keeper(z))
                def _():
                    wait_for(landed_factor.at[h, z], fa_recv.at[h, z])

        total = landed_factor[0, 0]
        for z in range(1, 2 * n):
            total += landed_factor[z // n, z % n]
        total = total.astype(BF16).astype(F32)
        for c in range(nc):
            blocks_out[c] = total[c * per_block : (c + 1) * per_block]
        every_other(lambda c, z: sketch_copy(c, z).start())
        landed_sketch[my_clip * count + me] = blocks_out[my_clip]

    @pl.loop(0, nc)
    def _(c):
        @pl.loop(0, count)
        def _(z):
            @pl.when((c != my_clip) | (z != me))
            def _():
                wait_for(landed_sketch.at[c * count + z], sk_recv.at[c * count + z])

    def partial_copy(c):
        return pltpu.make_async_remote_copy(
            src_ref=partial,
            dst_ref=landed_partial.at[my_clip],
            send_sem=pp_send.at[c],
            recv_sem=pp_recv.at[my_clip],
            device_id={"clip": c, "tensor": me},
            device_id_type=MESH,
        )

    def block_copy(c, q):
        return pltpu.make_async_remote_copy(
            src_ref=blocks.at[c, q],
            dst_ref=landed_blocks.at[me],
            send_sem=bl_send.at[c, q],
            recv_sem=bl_recv.at[me],
            device_id={"clip": c, "tensor": my_clip * ratio + q},
            device_id_type=MESH,
        )

    def other_clips(act):
        @pl.loop(0, nc)
        def _(c):
            @pl.when(c != my_clip)
            def _():
                act(c)

    load_hessian.wait()
    stacked = jnp.concatenate([landed_sketch[:, r, :] for r in range(per_block)], axis=1)
    partial[...] = jnp.dot(
        stacked.astype(BF16), hessian_ref[...], preferred_element_type=F32
    )
    other_clips(lambda c: partial_copy(c).start())
    landed_partial[my_clip] = partial[...]
    load_tests.wait()
    other_clips(lambda c: wait_for(landed_partial.at[c], pp_recv.at[c]))
    precond = landed_partial[0]
    for c in range(1, nc):
        precond += landed_partial[c]
    scores = lax.dot_general(
        precond.astype(BF16),
        tests_ref[...],
        (((1,), (1,)), ((), ())),
        preferred_element_type=F32,
    )
    for c in range(nc):
        for q in range(ratio):
            blocks[c, q] = scores[
                c * count : (c + 1) * count, q * out_width : (q + 1) * out_width
            ]

    def elsewhere(c, q):
        return (c != my_clip) | (my_clip * ratio + q != me)

    @pl.loop(0, nc)
    def _(c):
        @pl.loop(0, ratio)
        def _(q):
            @pl.when(elsewhere(c, q))
            def _():
                block_copy(c, q).start()

            @pl.when(jnp.logical_not(elsewhere(c, q)))
            def _():
                landed_blocks[me] = blocks[c, q]

    pair_copy(0, clips_ref).wait_send()
    pair_copy(1, targets_ref).wait_send()

    @pl.loop(0, steps)
    def _(k):
        def wait_part(k, first, size):
            @pl.when(me != keeper(k))
            def _():
                part_copy(k, first, size).wait_send()

        by_size(k, wait_part)

    @pl.loop(0, n)
    def _(j):
        @pl.when((j <= me) & (me < last))
        def _():
            wait_for(tok.at[j], ag_send.at[0, j])

        @pl.when((j >= me) & (me > 0))
        def _():
            wait_for(tok.at[j], ag_send.at[1, j])

        @pl.when(j != me)
        def _():
            wait_for(slots.at[j], rs_send.at[j])

    @pl.when(is_keeper(me))
    def _():
        other_factors(lambda h, c: factor_copy(h, c).wait_send())

    @pl.when(me < count)
    def _():
        every_other(lambda c, z: sketch_copy(c, z).wait_send())

    other_clips(lambda c: partial_copy(c).wait_send())

    holds_own = (me >= my_clip * ratio) & (me < (my_clip + 1) * ratio)

    @pl.loop(0, n)
    def _(z):
        @pl.when((z != me) | jnp.logical_not(holds_own))
        def _():
            wait_for(landed_blocks.at[z], bl_recv.at[z])

    total = landed_blocks[0]
    for z in range(1, n):
        total += landed_blocks[z]
    out_ref[...] = total

    @pl.loop(0, nc)
    def _(c):
        @pl.loop(0, ratio)
        def _(q):
            @pl.when(elsewhere(c, q))
            def _():
                block_copy(c, q).wait_send()


def agree_kernel(
    capacities, parts_n, nc, lengths_ref, index_ref, pair_ref, landed, send_sem, recv_sem
):
    my_clip = lax.axis_index("clip")
    mine = lax.axis_index("parts") * nc + my_clip
    count = lengths_ref.shape[0]
    groups = parts_n * nc

    def others(act):
        @pl.loop(0, parts_n)
        def _(y):
            @pl.loop(0, nc)
            def _(c):
                @pl.when(y * nc + c != mine)
                def _():
                    act(y, c)

    barrier = pltpu.get_barrier_semaphore()
    others(
        lambda y, c: pl.semaphore_signal(
            barrier, inc=1, device_id={"parts": y, "clip": c}, device_id_type=MESH
        )
    )
    sublane = lax.broadcasted_iota(jnp.int32, landed.shape[1:], 0)
    tile = jnp.zeros(landed.shape[1:], jnp.int32)
    for i in range(count):
        tile = jnp.where(sublane == i, lengths_ref[i], tile)
    landed[mine] = tile
    pl.semaphore_wait(barrier, groups - 1)

    def lengths_copy(y, c):
        return pltpu.make_async_remote_copy(
            src_ref=landed.at[mine],
            dst_ref=landed.at[mine],
            send_sem=send_sem.at[y * nc + c],
            recv_sem=recv_sem.at[mine],
            device_id={"parts": y, "clip": c},
            device_id_type=MESH,
        )

    others(lambda y, c: lengths_copy(y, c).start())
    others(
        lambda y, c: wait_for(landed.at[y * nc + c], recv_sem.at[y * nc + c])
    )
    most = jnp.zeros((1, landed.shape[2]), jnp.int32)
    for g in range(0, groups, 2):
        pair = landed[g] + landed[g + 1]
        total = pair[0:1]
        for i in range(1, count):
            total = total + pair[i : i + 1]
        most = jnp.maximum(most, total)
    index = jnp.zeros_like(most)
    for capacity in capacities[:-1]:
        index = index + jnp.where(most > 2 * capacity, 1, 0)
    index_ref[0] = jnp.max(index)
    start = mine - my_clip % 2
    pair_ref[0:count] = landed[start, 0:count]
    pair_ref[count:] = landed[start + 1, 0:count]
    others(lambda y, c: lengths_copy(y, c).wait_send())


def agree(capacities, parts_n, nc, lengths):
    count = lengths.shape[0]
    groups = parts_n * nc
    return pl.pallas_call(
        functools.partial(agree_kernel, capacities, parts_n, nc),
        out_shape=(
            jax.ShapeDtypeStruct((1,), jnp.int32),
            jax.ShapeDtypeStruct((2 * count, 128), jnp.int32),
        ),
        in_specs=[pl.BlockSpec(memory_space=pltpu.SMEM)],
        out_specs=(
            pl.BlockSpec(memory_space=pltpu.SMEM),
            pl.BlockSpec(memory_space=pltpu.VMEM),
        ),
        scratch_shapes=[
            pltpu.VMEM((groups, 8, 128), jnp.int32),
            pltpu.SemaphoreType.DMA((groups,)),
            pltpu.SemaphoreType.DMA((groups,)),
        ],
        compiler_params=pltpu.CompilerParams(collective_id=0, has_side_effects=True),
        name="agree",
    )(lengths)


def make_call(nc, n, sizes, rows, collective_id, args):
    clips, targets, lengths, gate, up, down, pin, pout, hessian, tests = args
    slots_all, width = clips.shape
    both_count = lengths.shape[0]
    count = both_count // 2
    hidden_part = gate.shape[1]
    proj = pin.shape[0]
    both = 2 * proj
    depth, columns = hessian.shape
    ratio = n // nc
    out_width = tests.shape[0] // ratio
    tile = 256 if hidden_part % 256 == 0 else hidden_part
    tile_w = 256 if width % 256 == 0 else width
    ahead = 3
    steps, pieces = len(sizes), 2 * len(sizes)
    total = sum(sizes) * rows
    rounds = -(-steps // n)
    vmem = pl.BlockSpec(memory_space=pltpu.VMEM)
    hbm = pl.BlockSpec(memory_space=pltpu.HBM)
    dma = pltpu.SemaphoreType.DMA
    tiles = width // tile_w
    return pl.pallas_call(
        functools.partial(scores_kernel, nc, n, sizes, rows, tile, ahead),
        out_shape=jax.ShapeDtypeStruct((count, out_width), F32),
        in_specs=[hbm, hbm, vmem] + [hbm] * 7,
        out_specs=vmem,
        scratch_shapes=[
            pltpu.VMEM((2, *clips.shape), BF16),
            pltpu.VMEM((2, *targets.shape), BF16),
            pltpu.VMEM((total, 128), jnp.int32),
            pltpu.VMEM((total, 128), jnp.int32),
            pltpu.VMEM((total, 128), F32),
            pltpu.VMEM(pin.shape, BF16),
            pltpu.VMEM((both, hidden_part), BF16),
            pltpu.VMEM((both, width), BF16),
            pltpu.VMEM(gate.shape, BF16),
            pltpu.VMEM(up.shape, BF16),
            pltpu.VMEM(down.shape, BF16),
            pltpu.VMEM((n, total, width), BF16),
            pltpu.VMEM((n + 1, tiles, total, tile_w), BF16),
            pltpu.VMEM((total, hidden_part), BF16),
            pltpu.VMEM((total, both), F32),
            pltpu.VMEM((rounds, n, max(sizes) * rows, both), F32),
            pltpu.VMEM((proj, both_count * both), F32),
            pltpu.VMEM((2, count, proj // 2, both), F32),
            pltpu.VMEM((2, n, proj // 2, both), F32),
            pltpu.VMEM((nc, depth // both, both), F32),
            pltpu.VMEM((nc * count, depth // both, both), F32),
            pltpu.VMEM((nc * count, columns), F32),
            pltpu.VMEM((nc, nc * count, columns), F32),
            pltpu.VMEM((nc, ratio, count, out_width), F32),
            pltpu.VMEM((n, count, out_width), F32),
            dma((9,)),
            dma((2,)),
            dma((2,)),
            dma((2, n)),
            dma((pieces, n)),
            dma((n,)),
            dma((steps, n + 1, tiles)),
            dma((steps,)),
            dma((rounds, n)),
            dma((2, count)),
            dma((2, n)),
            dma((nc, n)),
            dma((nc * count,)),
            dma((nc,)),
            dma((nc,)),
            dma((nc, ratio)),
            dma((n,)),
        ],
        compiler_params=pltpu.CompilerParams(
            collective_id=collective_id,
            has_side_effects=True,
            vmem_limit_bytes=63 * 1024 * 1024,
        ),
        cost_estimate=pl.CostEstimate(
            flops=6 * total * hidden_part * width * n,
            bytes_accessed=2 * 3 * hidden_part * width * n,
            transcendentals=total * hidden_part,
        ),
        name=f"influence_{total}",
    )


def on_device(parts_n, nc, n, *args):
    clips, targets, lengths = args[:3]
    count, clip_rows, width = clips.shape
    slots_all = count * clip_rows
    rows = 16
    full = slots_all // (4 * rows)
    plans = [(5, 6, 5, 5), (6, 6, 5, 5), (6, 6, 6, 5), (6, 6, 6, 6), (6, 7, 6, 6), (7, 7, 7, 6), (full,) * 4]
    capacities = [sum(sizes) * rows for sizes in plans]
    index, pair_lengths = agree(capacities, parts_n, nc, lengths)
    flat = (
        clips.reshape(slots_all, width),
        targets.reshape(slots_all, width),
        pair_lengths,
        *args[3:],
    )
    calls = [
        make_call(nc, n, sizes, rows, 1 + i, flat)
        for i, sizes in enumerate(plans)
    ]
    return lax.switch(index[0], calls, *flat)


def solution(mesh):
    in_specs = (
        P(("parts", "clip"), None, "tensor"),
        P(("parts", "clip"), None, "tensor"),
        P(("parts", "clip")),
        P(None, "tensor"),
        P(None, "tensor"),
        P("tensor", None),
        P(None, "tensor"),
        P(),
        P("clip", "tensor"),
        P("clip", "tensor"),
    )
    out_specs = P(("parts", "clip"), "tensor")
    return jax.shard_map(
        functools.partial(
            on_device, mesh.shape["parts"], mesh.shape["clip"], mesh.shape["tensor"]
        ),
        mesh=mesh,
        in_specs=in_specs,
        out_specs=out_specs,
        check_vma=False,
    )
```

```python
import functools

import jax
import jax.numpy as jnp
from jax import lax
from jax.experimental import pallas as pl
from jax.experimental.pallas import tpu as pltpu
from jax.sharding import PartitionSpec as P

MESH = pl.DeviceIdType.MESH
BF16, F32 = jnp.bfloat16, jnp.float32


def wait_for(ref, sem):
    pltpu.make_async_copy(ref, ref, sem).wait()


def scores_kernel(
    nc,
    n,
    sizes,
    rows,
    tile,
    ahead,
    clips_hbm,
    targets_hbm,
    lengths_ref,
    gate_hbm,
    up_hbm,
    down_hbm,
    pin_hbm,
    pout_hbm,
    hessian_hbm,
    tests_hbm,
    out_ref,
    clips_ref,
    targets_ref,
    source_ref,
    owner_ref,
    weight_ref,
    pin_raw,
    pin_ref,
    pout_ref,
    gate_ref,
    up_ref,
    down_ref,
    tok,
    slots,
    hid,
    joined,
    parts,
    product,
    factor,
    landed_factor,
    blocks_out,
    landed_sketch,
    partial,
    landed_partial,
    blocks,
    landed_blocks,
    load_sem,
    pair_send,
    pair_recv,
    ag_send,
    ag_recv,
    rs_send,
    rs_recv,
    own_send,
    own_recv,
    fa_send,
    fa_recv,
    sk_send,
    sk_recv,
    pp_send,
    pp_recv,
    bl_send,
    bl_recv,
):
    my_clip = lax.axis_index("clip")
    me = lax.axis_index("tensor")
    last = n - 1
    both_count = lengths_ref.shape[0]
    count = both_count // 2
    slots_all, width = clips_hbm.shape
    clip_rows = slots_all // count
    core = my_clip % 2
    other = my_clip + 1 - 2 * core
    lanes = lengths_ref.shape[1]
    base = sizes[0] * rows // count
    hidden_part = gate_ref.shape[1]
    proj = pin_hbm.shape[0]
    steps = len(sizes)
    cuts = [part for size in sizes for part in (size - size // 2, size // 2)]
    pieces = len(cuts)
    units = sum(sizes)
    tile_w = slots.shape[-1]
    tiles = width // tile_w

    def span(first, size):
        return pl.ds(pl.multiple_of(first * rows, rows), size * rows)

    def begin(k):
        return sum(jnp.where(k > i, size, 0) for i, size in enumerate(sizes))

    def piece_begin(m):
        return sum(jnp.where(m > i, size, 0) for i, size in enumerate(cuts))

    def by_length(lengths_of, start_of, k, act):
        for size in sorted(set(lengths_of)):
            same = [k == i for i, other_size in enumerate(lengths_of) if other_size == size]

            @pl.when(functools.reduce(jnp.logical_or, same))
            def _(size=size):
                act(k, start_of(k), size)

    by_size = functools.partial(by_length, sizes, begin)
    by_piece = functools.partial(by_length, cuts, piece_begin)
    depth, columns = hessian_hbm.shape
    tests_part = tests_hbm.shape[0]
    out_width = out_ref.shape[1]
    ratio = n // nc
    per_block = depth // (2 * proj)

    load_clips = pltpu.make_async_copy(clips_hbm, clips_ref.at[core], load_sem.at[0])
    load_clips.start()
    loads = [
        pltpu.make_async_copy(pin_hbm, pin_raw, load_sem.at[1]),
        pltpu.make_async_copy(gate_hbm, gate_ref, load_sem.at[2]),
        pltpu.make_async_copy(up_hbm, up_ref, load_sem.at[3]),
        pltpu.make_async_copy(down_hbm, down_ref, load_sem.at[4]),
        pltpu.make_async_copy(
            pout_hbm.at[:, pl.ds(pl.multiple_of(me * width, width), width)],
            pout_ref.at[pl.ds(proj, proj)],
            load_sem.at[5],
        ),
    ]
    load_targets = pltpu.make_async_copy(targets_hbm, targets_ref.at[core], load_sem.at[6])
    hessian_ref = gate_ref.at[pl.ds(0, depth), pl.ds(0, columns)]
    tests_ref = up_ref.at[pl.ds(0, tests_part), pl.ds(0, columns)]
    load_hessian = pltpu.make_async_copy(hessian_hbm, hessian_ref, load_sem.at[7])
    load_tests = pltpu.make_async_copy(tests_hbm, tests_ref, load_sem.at[8])

    barrier = pltpu.get_barrier_semaphore()

    @pl.loop(0, nc)
    def _(c):
        @pl.loop(0, n)
        def _(z):
            @pl.when((c != my_clip) | (z != me))
            def _():
                pl.semaphore_signal(
                    barrier, inc=1, device_id={"clip": c, "tensor": z}, device_id_type=MESH
                )

    pin_ref[proj:, :] = jnp.zeros((proj, hidden_part), BF16)
    pout_ref[:proj, :] = jnp.zeros((proj, width), BF16)

    lengths = [jnp.broadcast_to(lengths_ref[i : i + 1, :], (rows, lanes)) for i in range(both_count)]
    ends = []
    for length in lengths:
        ends.append(length - base + (ends[-1] if ends else 0))
    row = lax.broadcasted_iota(jnp.int32, (rows, lanes), 0)

    def save_table(m, source, owner, valid):
        length = lengths[0]
        for i in range(1, both_count):
            length = jnp.where(owner == i, lengths[i], length)
        where = span(m, 1)
        source_ref[where] = jnp.where(valid, source, -1)
        owner_ref[where] = jnp.where(valid, owner, -1)
        weight_ref[where] = jnp.where(valid, 1.0 / length.astype(F32), 0.0)

    def first_table(m):
        place = row + m * rows
        owner = jnp.zeros_like(row)
        for i in range(1, count):
            owner = owner + jnp.where(place >= i * base, 1, 0)
        source = owner * (clip_rows - base) + place
        save_table(m, source + core * slots_all, owner + core * count, row >= 0)

    def later_table(m):
        place = row + (core * (units - sizes[0]) + m - sizes[0]) * rows
        owner = jnp.zeros_like(row)
        source = place + base
        for i in range(both_count - 1):
            beyond = place >= ends[i]
            owner = owner + jnp.where(beyond, 1, 0)
            source = source + jnp.where(beyond, clip_rows + base - lengths[i], 0)
        save_table(m, source, owner, place < ends[-1])

    def pick(first, size, start, blocks_n):
        source = source_ref[span(first, size)] - start
        lane = lax.broadcasted_iota(jnp.int32, source.shape, 1)
        hits = [
            jnp.where(source == lane + b * lanes, 1.0, 0.0).astype(BF16) for b in range(blocks_n)
        ]
        return jnp.concatenate(hits, axis=1)

    def choose(chosen, ref, cols):
        return jnp.dot(
            chosen[:, :slots_all], ref[0, :, cols], preferred_element_type=F32
        ) + jnp.dot(chosen[:, slots_all:], ref[1, :, cols], preferred_element_type=F32)

    def pack_first():
        chosen = pick(0, sizes[0], core * slots_all, slots_all // lanes)

        @pl.loop(0, tiles)
        def _(t):
            cols = pl.ds(pl.multiple_of(t * tile_w, tile_w), tile_w)
            tok[me, span(0, sizes[0]), cols] = jnp.dot(
                chosen, clips_ref[core, :, cols], preferred_element_type=F32
            ).astype(BF16)

    def pack_later(k, first, size):
        chosen = pick(first, size, 0, 2 * slots_all // lanes)

        @pl.loop(0, tiles)
        def _(t):
            cols = pl.ds(pl.multiple_of(t * tile_w, tile_w), tile_w)
            tok[me, span(first, size), cols] = choose(chosen, clips_ref, cols).astype(BF16)

    def pair_copy(i, ref):
        return pltpu.make_async_remote_copy(
            src_ref=ref.at[core],
            dst_ref=ref.at[core],
            send_sem=pair_send.at[i],
            recv_sem=pair_recv.at[i],
            device_id={"clip": other},
            device_id_type=MESH,
        )


    @pl.loop(0, sizes[0])
    def _(m):
        first_table(m)

    load_clips.wait()
    load_targets.start()
    for load in loads:
        load.start()
    pack_first()
    pl.semaphore_wait(barrier, nc * n - 1)

    def token_copy(side, m, first, size, j):
        target = me + 1 if side == 0 else me - 1
        return pltpu.make_async_remote_copy(
            src_ref=tok.at[j, span(first, size)],
            dst_ref=tok.at[j, span(first, size)],
            send_sem=ag_send.at[side, j],
            recv_sem=ag_recv.at[m, j],
            device_id={"tensor": target},
            device_id_type=MESH,
        )

    def sum_copy(side, k, first, size, d, t):
        if side == 0:
            target, slot = me + 1, d
        else:
            target = me - 1
            slot = jnp.where(d == me - 1, n, d)
        return pltpu.make_async_remote_copy(
            src_ref=slots.at[d, t, span(first, size)],
            dst_ref=slots.at[slot, t, span(first, size)],
            send_sem=rs_send.at[d],
            recv_sem=rs_recv.at[k, slot, t],
            device_id={"tensor": target},
            device_id_type=MESH,
        )

    def send_own(m):
        def act(m, first, size):
            @pl.when(me < last)
            def _():
                token_copy(0, m, first, size, me).start()

            @pl.when(me > 0)
            def _():
                token_copy(1, m, first, size, me).start()

        by_piece(m, act)

    def gather_step(m):
        @pl.loop(1, n)
        def _(h):
            def act(q, first, size):
                @pl.when(me - h >= 0)
                def _():
                    wait_for(tok.at[me - h, span(first, size)], ag_recv.at[q, me - h])

                    @pl.when(me < last)
                    def _():
                        token_copy(0, q, first, size, me - h).start()

                @pl.when(me + h <= last)
                def _():
                    wait_for(tok.at[me + h, span(first, size)], ag_recv.at[q, me + h])

                    @pl.when(me > 0)
                    def _():
                        token_copy(1, q, first, size, me + h).start()

            by_piece(m - h, act)

        @pl.when(m + ahead < pieces)
        def _():
            send_own(m + ahead)

    def partial_tile(first, size, d, t):
        start = pl.multiple_of(d * width + t * tile_w, tile_w)
        return jnp.dot(
            hid[span(first, size)], down_ref[:, pl.ds(start, tile_w)], preferred_element_type=F32
        )

    def add_and_send(side, k, first, size, d):
        leading = me == (0 if side == 0 else last)

        @pl.loop(0, tiles)
        def _(t):
            where = span(first, size)

            @pl.when(leading)
            def _():
                slots[d, t, where] = partial_tile(first, size, d, t).astype(BF16)

            @pl.when(jnp.logical_not(leading))
            def _():
                mine = partial_tile(first, size, d, t)
                wait_for(slots.at[d, t, where], rs_recv.at[k, d, t])
                slots[d, t, where] = (mine + slots[d, t, where].astype(F32)).astype(BF16)

            sum_copy(side, k, first, size, d, t).start()

    def hidden_tile(first, size, t):
        cols = pl.ds(pl.multiple_of(t * tile, tile), tile)
        gate_act = jnp.zeros((size * rows, tile), F32)
        up_act = jnp.zeros((size * rows, tile), F32)
        for j in range(n):
            piece = tok[j, span(first, size)]
            part = slice(j * width, (j + 1) * width)
            gate_act += jnp.dot(piece, gate_ref[part, cols], preferred_element_type=F32)
            up_act += jnp.dot(piece, up_ref[part, cols], preferred_element_type=F32)
        silu = gate_act / (1.0 + jnp.exp(-gate_act))
        hid[span(first, size), cols] = (silu * up_act).astype(BF16)

    def join_left(first, size):
        joined[span(first, size)] = lax.dot_general(
            hid[span(first, size)],
            pin_ref[...],
            (((1,), (1,)), ((), ())),
            preferred_element_type=F32,
        )

    shift = (n + n // 2 - steps) % n

    def keeper(k):
        return (k + shift) % n

    kept = (me + n - shift) % n

    def part_copy(k, first, size):
        return pltpu.make_async_remote_copy(
            src_ref=joined.at[span(first, size)],
            dst_ref=parts.at[k // n, me, pl.ds(0, size * rows)],
            send_sem=own_send.at[k],
            recv_sem=own_recv.at[k // n, me],
            device_id={"tensor": keeper(k)},
            device_id_type=MESH,
        )

    def finish(k, first, size):
        shape = (size * rows, tile_w)
        has_left = jnp.full(shape, jnp.where(me > 0, 1.0, 0.0), F32) > 0.5
        has_right = jnp.full(shape, jnp.where(me < last, 1.0, 0.0), F32) > 0.5
        where = span(first, size)
        weight = jnp.concatenate([weight_ref[where]] * (tile_w // lanes), axis=1)
        chosen = pick(first, size, 0, 2 * slots_all // lanes)

        @pl.loop(0, tiles)
        def _(t):
            cols = pl.ds(pl.multiple_of(t * tile_w, tile_w), tile_w)
            total = partial_tile(first, size, me, t)
            golden = choose(chosen, targets_ref, cols)

            @pl.when(me > 0)
            def _():
                wait_for(slots.at[me, t, where], rs_recv.at[k, me, t])

            @pl.when(me < last)
            def _():
                wait_for(slots.at[n, t, where], rs_recv.at[k, n, t])

            total += jnp.where(has_left, slots[me, t, where].astype(F32), 0.0)
            total += jnp.where(has_right, slots[n, t, where].astype(F32), 0.0)
            differ = jnp.clip(total - golden, -1.0, 1.0)
            grad = (differ * weight).astype(BF16)
            joined[where] += lax.dot_general(
                grad, pout_ref[:, cols], (((1,), (1,)), ((), ())), preferred_element_type=F32
            )

        @pl.when(me != keeper(k))
        def _():
            part_copy(k, first, size).start()

    @pl.loop(0, 2)
    def _(m):
        send_own(m)

    pair_copy(0, clips_ref).start()

    @pl.loop(sizes[0], units)
    def _(m):
        later_table(m)

    load_targets.wait()
    pair_copy(1, targets_ref).start()
    wait_for(clips_ref.at[1 - core], pair_recv.at[0])

    @pl.loop(1, steps)
    def _(k):
        by_size(k, pack_later)

    @pl.loop(2, ahead)
    def _(m):
        send_own(m)

    @pl.loop(0, 2 + last)
    def _(m):
        gather_step(m)

    loads[0].wait()
    order_row = lax.broadcasted_iota(jnp.int32, (proj, proj), 0)
    order_col = lax.broadcasted_iota(jnp.int32, (proj, proj), 1)
    half = proj // 2
    wanted = jnp.where(order_row < half, 2 * order_row, 2 * (order_row - half) + 1)
    shuffle = jnp.where(order_col == wanted, 1.0, 0.0).astype(BF16)
    pin_ref[:proj, :] = jnp.dot(shuffle, pin_raw[...], preferred_element_type=F32).astype(BF16)

    hidden_tiles = hidden_part // tile

    @pl.loop(0, steps + last)
    def _(k):
        upto = 2 * (k + 1) + last

        def more(i):
            @pl.when(upto + i < pieces + last)
            def _():
                gather_step(upto + i)

        @pl.when(k == 0)
        def _():
            loads[1].wait()
            loads[2].wait()

        def make_hidden(k, first, size):
            @pl.loop(0, hidden_tiles)
            def _(t):
                hidden_tile(first, size, t)

            join_left(first, size)

        by_size(k, make_hidden)

        @pl.when(k == steps - 1)
        def _():
            load_hessian.start()
            load_tests.start()

        @pl.when(k == 0)
        def _():
            for load in loads[3:]:
                load.wait()
            wait_for(targets_ref.at[1 - core], pair_recv.at[1])

        more(0)

        def send_right(k, first, size):
            @pl.loop(0, last - me)
            def _(i):
                add_and_send(0, k, first, size, last - i)

        by_size(k - me, send_right)

        def send_left(k, first, size):
            @pl.loop(0, me)
            def _(d):
                add_and_send(1, k, first, size, d)

        by_size(k - (last - me), send_left)
        by_size(k - last, finish)
        more(1)

    pair_start = my_clip - core

    def factor_copy(h, c):
        return pltpu.make_async_remote_copy(
            src_ref=factor.at[h, c],
            dst_ref=landed_factor.at[core, me],
            send_sem=fa_send.at[h, c],
            recv_sem=fa_recv.at[core, me],
            device_id={"clip": pair_start + h, "tensor": c},
            device_id_type=MESH,
        )

    def other_factors(act):
        @pl.loop(0, 2)
        def _(h):
            @pl.loop(0, count)
            def _(c):
                @pl.when((h != core) | (c != me))
                def _():
                    act(h, c)

    def add_product(k, first, size):
        held = pl.ds(0, size * rows)
        total = joined[span(first, size)]

        @pl.loop(0, n)
        def _(j):
            @pl.when(j != me)
            def _():
                wait_for(parts.at[k // n, j, held], own_recv.at[k // n, j])

        parts[k // n, me, held] = total
        total = parts[k // n, 0, held]
        for j in range(1, n):
            total += parts[k // n, j, held]
        lane = lax.broadcasted_iota(jnp.int32, total.shape, 1)
        right = jnp.where(lane < proj, pltpu.roll(total, proj, 1), total)
        owner = owner_ref[span(first, size)]
        product[...] += jnp.dot(
            total.T[:proj],
            jnp.concatenate(
                [jnp.where(owner == i, right, 0.0) for i in range(both_count)], axis=1
            ),
            precision=lax.Precision.HIGHEST,
            preferred_element_type=F32,
        )

    def is_keeper(z):
        return (z + n - shift) % n < steps

    @pl.when(is_keeper(me))
    def _():
        product[...] = jnp.zeros_like(product)
        for i in range(parts.shape[0]):
            by_size(kept + i * n, add_product)
        low = lax.broadcasted_iota(jnp.int32, (half, 2 * proj), 1) < proj
        for i in range(both_count):
            cols = slice(i * 2 * proj, (i + 1) * 2 * proj)
            factor[i // count, i % count] = jnp.where(
                low, product[:half, cols], product[half:, cols]
            )
        other_factors(lambda h, c: factor_copy(h, c).start())

    def sketch_copy(c, z):
        return pltpu.make_async_remote_copy(
            src_ref=blocks_out.at[c],
            dst_ref=landed_sketch.at[my_clip * count + me],
            send_sem=sk_send.at[c, z],
            recv_sem=sk_recv.at[my_clip * count + me],
            device_id={"clip": c, "tensor": z},
            device_id_type=MESH,
        )

    def every_other(act):
        @pl.loop(0, nc)
        def _(c):
            @pl.loop(0, n)
            def _(z):
                @pl.when((c != my_clip) | (z != me))
                def _():
                    act(c, z)

    @pl.when(me < count)
    def _():
        @pl.when(is_keeper(me))
        def _():
            landed_factor[core, me] = factor[core, me]

        if steps < n:
            @pl.loop(0, n)
            def _(z):
                @pl.when(jnp.logical_not(is_keeper(z)))
                def _():
                    landed_factor[0, z] = jnp.zeros_like(landed_factor[0, z])
                    landed_factor[1, z] = jnp.zeros_like(landed_factor[1, z])

        @pl.loop(0, 2)
        def _(h):
            @pl.loop(0, n)
            def _(z):
                @pl.when(((h != core) | (z != me)) & is_keeper(z))
                def _():
                    wait_for(landed_factor.at[h, z], fa_recv.at[h, z])

        total = landed_factor[0, 0]
        for z in range(1, 2 * n):
            total += landed_factor[z // n, z % n]
        total = total.astype(BF16).astype(F32)
        for c in range(nc):
            blocks_out[c] = total[c * per_block : (c + 1) * per_block]
        every_other(lambda c, z: sketch_copy(c, z).start())
        landed_sketch[my_clip * count + me] = blocks_out[my_clip]

    @pl.loop(0, nc)
    def _(c):
        @pl.loop(0, count)
        def _(z):
            @pl.when((c != my_clip) | (z != me))
            def _():
                wait_for(landed_sketch.at[c * count + z], sk_recv.at[c * count + z])

    def partial_copy(c):
        return pltpu.make_async_remote_copy(
            src_ref=partial,
            dst_ref=landed_partial.at[my_clip],
            send_sem=pp_send.at[c],
            recv_sem=pp_recv.at[my_clip],
            device_id={"clip": c, "tensor": me},
            device_id_type=MESH,
        )

    def block_copy(c, q):
        return pltpu.make_async_remote_copy(
            src_ref=blocks.at[c, q],
            dst_ref=landed_blocks.at[me],
            send_sem=bl_send.at[c, q],
            recv_sem=bl_recv.at[me],
            device_id={"clip": c, "tensor": my_clip * ratio + q},
            device_id_type=MESH,
        )

    def other_clips(act):
        @pl.loop(0, nc)
        def _(c):
            @pl.when(c != my_clip)
            def _():
                act(c)

    load_hessian.wait()
    stacked = jnp.concatenate([landed_sketch[:, r, :] for r in range(per_block)], axis=1)
    partial[...] = jnp.dot(
        stacked.astype(BF16), hessian_ref[...], preferred_element_type=F32
    )
    other_clips(lambda c: partial_copy(c).start())
    landed_partial[my_clip] = partial[...]
    load_tests.wait()
    other_clips(lambda c: wait_for(landed_partial.at[c], pp_recv.at[c]))
    precond = landed_partial[0]
    for c in range(1, nc):
        precond += landed_partial[c]
    scores = lax.dot_general(
        precond.astype(BF16),
        tests_ref[...],
        (((1,), (1,)), ((), ())),
        preferred_element_type=F32,
    )
    for c in range(nc):
        for q in range(ratio):
            blocks[c, q] = scores[
                c * count : (c + 1) * count, q * out_width : (q + 1) * out_width
            ]

    def elsewhere(c, q):
        return (c != my_clip) | (my_clip * ratio + q != me)

    @pl.loop(0, nc)
    def _(c):
        @pl.loop(0, ratio)
        def _(q):
            @pl.when(elsewhere(c, q))
            def _():
                block_copy(c, q).start()

            @pl.when(jnp.logical_not(elsewhere(c, q)))
            def _():
                landed_blocks[me] = blocks[c, q]

    pair_copy(0, clips_ref).wait_send()
    pair_copy(1, targets_ref).wait_send()

    @pl.loop(0, steps)
    def _(k):
        def wait_part(k, first, size):
            @pl.when(me != keeper(k))
            def _():
                part_copy(k, first, size).wait_send()

        by_size(k, wait_part)

    @pl.loop(0, n)
    def _(j):
        @pl.when((j <= me) & (me < last))
        def _():
            wait_for(tok.at[j], ag_send.at[0, j])

        @pl.when((j >= me) & (me > 0))
        def _():
            wait_for(tok.at[j], ag_send.at[1, j])

        @pl.when(j != me)
        def _():
            wait_for(slots.at[j], rs_send.at[j])

    @pl.when(is_keeper(me))
    def _():
        other_factors(lambda h, c: factor_copy(h, c).wait_send())

    @pl.when(me < count)
    def _():
        every_other(lambda c, z: sketch_copy(c, z).wait_send())

    other_clips(lambda c: partial_copy(c).wait_send())

    holds_own = (me >= my_clip * ratio) & (me < (my_clip + 1) * ratio)

    @pl.loop(0, n)
    def _(z):
        @pl.when((z != me) | jnp.logical_not(holds_own))
        def _():
            wait_for(landed_blocks.at[z], bl_recv.at[z])

    total = landed_blocks[0]
    for z in range(1, n):
        total += landed_blocks[z]
    out_ref[...] = total

    @pl.loop(0, nc)
    def _(c):
        @pl.loop(0, ratio)
        def _(q):
            @pl.when(elsewhere(c, q))
            def _():
                block_copy(c, q).wait_send()


def agree_kernel(
    capacities, parts_n, nc, lengths_ref, index_ref, pair_ref, landed, send_sem, recv_sem
):
    my_clip = lax.axis_index("clip")
    mine = lax.axis_index("parts") * nc + my_clip
    count = lengths_ref.shape[0]
    groups = parts_n * nc

    def others(act):
        @pl.loop(0, parts_n)
        def _(y):
            @pl.loop(0, nc)
            def _(c):
                @pl.when(y * nc + c != mine)
                def _():
                    act(y, c)

    barrier = pltpu.get_barrier_semaphore()
    others(
        lambda y, c: pl.semaphore_signal(
            barrier, inc=1, device_id={"parts": y, "clip": c}, device_id_type=MESH
        )
    )
    sublane = lax.broadcasted_iota(jnp.int32, landed.shape[1:], 0)
    tile = jnp.zeros(landed.shape[1:], jnp.int32)
    for i in range(count):
        tile = jnp.where(sublane == i, lengths_ref[i], tile)
    landed[mine] = tile
    pl.semaphore_wait(barrier, groups - 1)

    def lengths_copy(y, c):
        return pltpu.make_async_remote_copy(
            src_ref=landed.at[mine],
            dst_ref=landed.at[mine],
            send_sem=send_sem.at[y * nc + c],
            recv_sem=recv_sem.at[mine],
            device_id={"parts": y, "clip": c},
            device_id_type=MESH,
        )

    others(lambda y, c: lengths_copy(y, c).start())
    others(
        lambda y, c: wait_for(landed.at[y * nc + c], recv_sem.at[y * nc + c])
    )
    most = jnp.zeros((1, landed.shape[2]), jnp.int32)
    for g in range(0, groups, 2):
        pair = landed[g] + landed[g + 1]
        total = pair[0:1]
        for i in range(1, count):
            total = total + pair[i : i + 1]
        most = jnp.maximum(most, total)
    index = jnp.zeros_like(most)
    for capacity in capacities[:-1]:
        index = index + jnp.where(most > 2 * capacity, 1, 0)
    index_ref[0] = jnp.max(index)
    start = mine - my_clip % 2
    pair_ref[0:count] = landed[start, 0:count]
    pair_ref[count:] = landed[start + 1, 0:count]
    others(lambda y, c: lengths_copy(y, c).wait_send())


def agree(capacities, parts_n, nc, lengths):
    count = lengths.shape[0]
    groups = parts_n * nc
    return pl.pallas_call(
        functools.partial(agree_kernel, capacities, parts_n, nc),
        out_shape=(
            jax.ShapeDtypeStruct((1,), jnp.int32),
            jax.ShapeDtypeStruct((2 * count, 128), jnp.int32),
        ),
        in_specs=[pl.BlockSpec(memory_space=pltpu.SMEM)],
        out_specs=(
            pl.BlockSpec(memory_space=pltpu.SMEM),
            pl.BlockSpec(memory_space=pltpu.VMEM),
        ),
        scratch_shapes=[
            pltpu.VMEM((groups, 8, 128), jnp.int32),
            pltpu.SemaphoreType.DMA((groups,)),
            pltpu.SemaphoreType.DMA((groups,)),
        ],
        compiler_params=pltpu.CompilerParams(collective_id=0, has_side_effects=True),
        name="agree",
    )(lengths)


def make_call(nc, n, sizes, rows, collective_id, args):
    clips, targets, lengths, gate, up, down, pin, pout, hessian, tests = args
    slots_all, width = clips.shape
    both_count = lengths.shape[0]
    count = both_count // 2
    hidden_part = gate.shape[1]
    proj = pin.shape[0]
    both = 2 * proj
    depth, columns = hessian.shape
    ratio = n // nc
    out_width = tests.shape[0] // ratio
    tile = 256 if hidden_part % 256 == 0 else hidden_part
    tile_w = 256 if width % 256 == 0 else width
    ahead = 3
    steps, pieces = len(sizes), 2 * len(sizes)
    total = sum(sizes) * rows
    rounds = -(-steps // n)
    vmem = pl.BlockSpec(memory_space=pltpu.VMEM)
    hbm = pl.BlockSpec(memory_space=pltpu.HBM)
    dma = pltpu.SemaphoreType.DMA
    tiles = width // tile_w
    return pl.pallas_call(
        functools.partial(scores_kernel, nc, n, sizes, rows, tile, ahead),
        out_shape=jax.ShapeDtypeStruct((count, out_width), F32),
        in_specs=[hbm, hbm, vmem] + [hbm] * 7,
        out_specs=vmem,
        scratch_shapes=[
            pltpu.VMEM((2, *clips.shape), BF16),
            pltpu.VMEM((2, *targets.shape), BF16),
            pltpu.VMEM((total, 128), jnp.int32),
            pltpu.VMEM((total, 128), jnp.int32),
            pltpu.VMEM((total, 128), F32),
            pltpu.VMEM(pin.shape, BF16),
            pltpu.VMEM((both, hidden_part), BF16),
            pltpu.VMEM((both, width), BF16),
            pltpu.VMEM(gate.shape, BF16),
            pltpu.VMEM(up.shape, BF16),
            pltpu.VMEM(down.shape, BF16),
            pltpu.VMEM((n, total, width), BF16),
            pltpu.VMEM((n + 1, tiles, total, tile_w), BF16),
            pltpu.VMEM((total, hidden_part), BF16),
            pltpu.VMEM((total, both), F32),
            pltpu.VMEM((rounds, n, max(sizes) * rows, both), F32),
            pltpu.VMEM((proj, both_count * both), F32),
            pltpu.VMEM((2, count, proj // 2, both), F32),
            pltpu.VMEM((2, n, proj // 2, both), F32),
            pltpu.VMEM((nc, depth // both, both), F32),
            pltpu.VMEM((nc * count, depth // both, both), F32),
            pltpu.VMEM((nc * count, columns), F32),
            pltpu.VMEM((nc, nc * count, columns), F32),
            pltpu.VMEM((nc, ratio, count, out_width), F32),
            pltpu.VMEM((n, count, out_width), F32),
            dma((9,)),
            dma((2,)),
            dma((2,)),
            dma((2, n)),
            dma((pieces, n)),
            dma((n,)),
            dma((steps, n + 1, tiles)),
            dma((steps,)),
            dma((rounds, n)),
            dma((2, count)),
            dma((2, n)),
            dma((nc, n)),
            dma((nc * count,)),
            dma((nc,)),
            dma((nc,)),
            dma((nc, ratio)),
            dma((n,)),
        ],
        compiler_params=pltpu.CompilerParams(
            collective_id=collective_id,
            has_side_effects=True,
            vmem_limit_bytes=63 * 1024 * 1024,
        ),
        cost_estimate=pl.CostEstimate(
            flops=6 * total * hidden_part * width * n,
            bytes_accessed=2 * 3 * hidden_part * width * n,
            transcendentals=total * hidden_part,
        ),
        name=f"influence_{total}",
    )


def on_device(parts_n, nc, n, *args):
    clips, targets, lengths = args[:3]
    count, clip_rows, width = clips.shape
    slots_all = count * clip_rows
    rows = 16
    full = slots_all // (4 * rows)
    plans = [(6, 6, 5, 5), (6, 6, 6, 6), (7, 7, 6, 6), (full,) * 4]
    capacities = [sum(sizes) * rows for sizes in plans]
    index, pair_lengths = agree(capacities, parts_n, nc, lengths)
    flat = (
        clips.reshape(slots_all, width),
        targets.reshape(slots_all, width),
        pair_lengths,
        *args[3:],
    )
    calls = [
        make_call(nc, n, sizes, rows, 1 + i, flat)
        for i, sizes in enumerate(plans)
    ]
    return lax.switch(index[0], calls, *flat)


def solution(mesh):
    in_specs = (
        P(("parts", "clip"), None, "tensor"),
        P(("parts", "clip"), None, "tensor"),
        P(("parts", "clip")),
        P(None, "tensor"),
        P(None, "tensor"),
        P("tensor", None),
        P(None, "tensor"),
        P(),
        P("clip", "tensor"),
        P("clip", "tensor"),
    )
    out_specs = P(("parts", "clip"), "tensor")
    return jax.shard_map(
        functools.partial(
            on_device, mesh.shape["parts"], mesh.shape["clip"], mesh.shape["tensor"]
        ),
        mesh=mesh,
        in_specs=in_specs,
        out_specs=out_specs,
        check_vma=False,
    )
```

```python
import functools

import jax
import jax.numpy as jnp
from jax import lax
from jax.experimental import pallas as pl
from jax.experimental.pallas import tpu as pltpu
from jax.sharding import PartitionSpec as P

MESH = pl.DeviceIdType.MESH
BF16, F32 = jnp.bfloat16, jnp.float32


def wait_for(ref, sem):
    pltpu.make_async_copy(ref, ref, sem).wait()


def scores_kernel(
    nc,
    n,
    sizes,
    rows,
    tile,
    ahead,
    clips_hbm,
    targets_hbm,
    lengths_ref,
    gate_hbm,
    up_hbm,
    down_hbm,
    pin_hbm,
    pout_hbm,
    hessian_hbm,
    tests_hbm,
    out_ref,
    clips_ref,
    targets_ref,
    source_ref,
    owner_ref,
    weight_ref,
    pin_raw,
    pin_ref,
    pout_ref,
    gate_ref,
    up_ref,
    down_ref,
    tok,
    slots,
    hid,
    joined,
    parts,
    product,
    factor,
    landed_factor,
    blocks_out,
    landed_sketch,
    partial,
    landed_partial,
    blocks,
    landed_blocks,
    load_sem,
    pair_send,
    pair_recv,
    ag_send,
    ag_recv,
    rs_send,
    rs_recv,
    own_send,
    own_recv,
    fa_send,
    fa_recv,
    sk_send,
    sk_recv,
    pp_send,
    pp_recv,
    bl_send,
    bl_recv,
):
    my_clip = lax.axis_index("clip")
    me = lax.axis_index("tensor")
    last = n - 1
    both_count = lengths_ref.shape[0]
    count = both_count // 2
    slots_all, width = clips_hbm.shape
    clip_rows = slots_all // count
    core = my_clip % 2
    other = my_clip + 1 - 2 * core
    lanes = lengths_ref.shape[1]
    base = sizes[0] * rows // count
    hidden_part = gate_ref.shape[1]
    proj = pin_hbm.shape[0]
    steps = len(sizes)
    cuts = [part for size in sizes for part in (size - size // 2, size // 2)]
    pieces = len(cuts)
    units = sum(sizes)
    tile_w = slots.shape[-1]
    tiles = width // tile_w

    def span(first, size):
        return pl.ds(pl.multiple_of(first * rows, rows), size * rows)

    def begin(k):
        return sum(jnp.where(k > i, size, 0) for i, size in enumerate(sizes))

    def piece_begin(m):
        return sum(jnp.where(m > i, size, 0) for i, size in enumerate(cuts))

    def by_length(lengths_of, start_of, k, act):
        for size in sorted(set(lengths_of)):
            same = [k == i for i, other_size in enumerate(lengths_of) if other_size == size]

            @pl.when(functools.reduce(jnp.logical_or, same))
            def _(size=size):
                act(k, start_of(k), size)

    by_size = functools.partial(by_length, sizes, begin)
    by_piece = functools.partial(by_length, cuts, piece_begin)
    depth, columns = hessian_hbm.shape
    tests_part = tests_hbm.shape[0]
    out_width = out_ref.shape[1]
    ratio = n // nc
    per_block = depth // (2 * proj)

    load_clips = pltpu.make_async_copy(clips_hbm, clips_ref.at[core], load_sem.at[0])
    load_clips.start()
    loads = [
        pltpu.make_async_copy(pin_hbm, pin_raw, load_sem.at[1]),
        pltpu.make_async_copy(gate_hbm, gate_ref, load_sem.at[2]),
        pltpu.make_async_copy(up_hbm, up_ref, load_sem.at[3]),
        pltpu.make_async_copy(down_hbm, down_ref, load_sem.at[4]),
        pltpu.make_async_copy(
            pout_hbm.at[:, pl.ds(pl.multiple_of(me * width, width), width)],
            pout_ref.at[pl.ds(proj, proj)],
            load_sem.at[5],
        ),
    ]
    load_targets = pltpu.make_async_copy(targets_hbm, targets_ref.at[core], load_sem.at[6])
    hessian_ref = gate_ref.at[pl.ds(0, depth), pl.ds(0, columns)]
    tests_ref = up_ref.at[pl.ds(0, tests_part), pl.ds(0, columns)]
    load_hessian = pltpu.make_async_copy(hessian_hbm, hessian_ref, load_sem.at[7])
    load_tests = pltpu.make_async_copy(tests_hbm, tests_ref, load_sem.at[8])

    barrier = pltpu.get_barrier_semaphore()

    @pl.loop(0, nc)
    def _(c):
        @pl.loop(0, n)
        def _(z):
            @pl.when((c != my_clip) | (z != me))
            def _():
                pl.semaphore_signal(
                    barrier, inc=1, device_id={"clip": c, "tensor": z}, device_id_type=MESH
                )

    pin_ref[proj:, :] = jnp.zeros((proj, hidden_part), BF16)
    pout_ref[:proj, :] = jnp.zeros((proj, width), BF16)

    lengths = [jnp.broadcast_to(lengths_ref[i : i + 1, :], (rows, lanes)) for i in range(both_count)]
    ends = []
    for length in lengths:
        ends.append(length - base + (ends[-1] if ends else 0))
    row = lax.broadcasted_iota(jnp.int32, (rows, lanes), 0)

    def save_table(m, source, owner, valid):
        length = lengths[0]
        for i in range(1, both_count):
            length = jnp.where(owner == i, lengths[i], length)
        where = span(m, 1)
        source_ref[where] = jnp.where(valid, source, -1)
        owner_ref[where] = jnp.where(valid, owner, -1)
        weight_ref[where] = jnp.where(valid, 1.0 / length.astype(F32), 0.0)

    def first_table(m):
        place = row + m * rows
        owner = jnp.zeros_like(row)
        for i in range(1, count):
            owner = owner + jnp.where(place >= i * base, 1, 0)
        source = owner * (clip_rows - base) + place
        save_table(m, source + core * slots_all, owner + core * count, row >= 0)

    def later_table(m):
        place = row + (core * (units - sizes[0]) + m - sizes[0]) * rows
        owner = jnp.zeros_like(row)
        source = place + base
        for i in range(both_count - 1):
            beyond = place >= ends[i]
            owner = owner + jnp.where(beyond, 1, 0)
            source = source + jnp.where(beyond, clip_rows + base - lengths[i], 0)
        save_table(m, source, owner, place < ends[-1])

    def pick(first, size, start, blocks_n):
        source = source_ref[span(first, size)] - start
        lane = lax.broadcasted_iota(jnp.int32, source.shape, 1)
        hits = [
            jnp.where(source == lane + b * lanes, 1.0, 0.0).astype(BF16) for b in range(blocks_n)
        ]
        return jnp.concatenate(hits, axis=1)

    def choose(chosen, ref, cols):
        return jnp.dot(
            chosen[:, :slots_all], ref[0, :, cols], preferred_element_type=F32
        ) + jnp.dot(chosen[:, slots_all:], ref[1, :, cols], preferred_element_type=F32)

    def pack_first():
        chosen = pick(0, sizes[0], core * slots_all, slots_all // lanes)

        @pl.loop(0, tiles)
        def _(t):
            cols = pl.ds(pl.multiple_of(t * tile_w, tile_w), tile_w)
            tok[me, span(0, sizes[0]), cols] = jnp.dot(
                chosen, clips_ref[core, :, cols], preferred_element_type=F32
            ).astype(BF16)

    def pack_later(k, first, size):
        chosen = pick(first, size, 0, 2 * slots_all // lanes)

        @pl.loop(0, tiles)
        def _(t):
            cols = pl.ds(pl.multiple_of(t * tile_w, tile_w), tile_w)
            tok[me, span(first, size), cols] = choose(chosen, clips_ref, cols).astype(BF16)

    def pair_copy(i, ref):
        return pltpu.make_async_remote_copy(
            src_ref=ref.at[core],
            dst_ref=ref.at[core],
            send_sem=pair_send.at[i],
            recv_sem=pair_recv.at[i],
            device_id={"clip": other},
            device_id_type=MESH,
        )


    @pl.loop(0, sizes[0])
    def _(m):
        first_table(m)

    load_clips.wait()
    load_targets.start()
    for load in loads:
        load.start()
    pack_first()
    pl.semaphore_wait(barrier, nc * n - 1)

    def token_copy(side, m, first, size, j):
        target = me + 1 if side == 0 else me - 1
        return pltpu.make_async_remote_copy(
            src_ref=tok.at[j, span(first, size)],
            dst_ref=tok.at[j, span(first, size)],
            send_sem=ag_send.at[side, j],
            recv_sem=ag_recv.at[m, j],
            device_id={"tensor": target},
            device_id_type=MESH,
        )

    def sum_copy(side, k, first, size, d, t):
        if side == 0:
            target, slot = me + 1, d
        else:
            target = me - 1
            slot = jnp.where(d == me - 1, n, d)
        return pltpu.make_async_remote_copy(
            src_ref=slots.at[d, t, span(first, size)],
            dst_ref=slots.at[slot, t, span(first, size)],
            send_sem=rs_send.at[d],
            recv_sem=rs_recv.at[k, slot, t],
            device_id={"tensor": target},
            device_id_type=MESH,
        )

    def send_own(m):
        def act(m, first, size):
            @pl.when(me < last)
            def _():
                token_copy(0, m, first, size, me).start()

            @pl.when(me > 0)
            def _():
                token_copy(1, m, first, size, me).start()

        by_piece(m, act)

    def forward(m):
        @pl.loop(1, n)
        def _(h):
            def act(q, first, size):
                @pl.when(me - h >= 0)
                def _():
                    wait_for(tok.at[me - h, span(first, size)], ag_recv.at[q, me - h])

                    @pl.when(me < last)
                    def _():
                        token_copy(0, q, first, size, me - h).start()

                @pl.when(me + h <= last)
                def _():
                    wait_for(tok.at[me + h, span(first, size)], ag_recv.at[q, me + h])

                    @pl.when(me > 0)
                    def _():
                        token_copy(1, q, first, size, me + h).start()

            by_piece(m - h, act)

    def gather_step(m):
        forward(m)

        @pl.when(m + ahead < pieces)
        def _():
            send_own(m + ahead)

    def partial_tile(first, size, d, t):
        start = pl.multiple_of(d * width + t * tile_w, tile_w)
        return jnp.dot(
            hid[span(first, size)], down_ref[:, pl.ds(start, tile_w)], preferred_element_type=F32
        )

    def add_and_send(side, k, first, size, d):
        leading = me == (0 if side == 0 else last)

        @pl.loop(0, tiles)
        def _(t):
            where = span(first, size)

            @pl.when(leading)
            def _():
                slots[d, t, where] = partial_tile(first, size, d, t).astype(BF16)

            @pl.when(jnp.logical_not(leading))
            def _():
                mine = partial_tile(first, size, d, t)
                wait_for(slots.at[d, t, where], rs_recv.at[k, d, t])
                slots[d, t, where] = (mine + slots[d, t, where].astype(F32)).astype(BF16)

            sum_copy(side, k, first, size, d, t).start()

    def hidden_tile(first, size, t):
        cols = pl.ds(pl.multiple_of(t * tile, tile), tile)
        gate_act = jnp.zeros((size * rows, tile), F32)
        up_act = jnp.zeros((size * rows, tile), F32)
        for j in range(n):
            piece = tok[j, span(first, size)]
            part = slice(j * width, (j + 1) * width)
            gate_act += jnp.dot(piece, gate_ref[part, cols], preferred_element_type=F32)
            up_act += jnp.dot(piece, up_ref[part, cols], preferred_element_type=F32)
        silu = gate_act / (1.0 + jnp.exp(-gate_act))
        hid[span(first, size), cols] = (silu * up_act).astype(BF16)

    def join_left(first, size):
        joined[span(first, size)] = lax.dot_general(
            hid[span(first, size)],
            pin_ref[...],
            (((1,), (1,)), ((), ())),
            preferred_element_type=F32,
        )

    shift = (n + n // 2 - steps) % n

    def keeper(k):
        return (k + shift) % n

    kept = (me + n - shift) % n

    def part_copy(k, first, size):
        return pltpu.make_async_remote_copy(
            src_ref=joined.at[span(first, size)],
            dst_ref=parts.at[k // n, me, pl.ds(0, size * rows)],
            send_sem=own_send.at[k],
            recv_sem=own_recv.at[k // n, me],
            device_id={"tensor": keeper(k)},
            device_id_type=MESH,
        )

    def finish(k, first, size):
        shape = (size * rows, tile_w)
        has_left = jnp.full(shape, jnp.where(me > 0, 1.0, 0.0), F32) > 0.5
        has_right = jnp.full(shape, jnp.where(me < last, 1.0, 0.0), F32) > 0.5
        where = span(first, size)
        weight = jnp.concatenate([weight_ref[where]] * (tile_w // lanes), axis=1)
        chosen = pick(first, size, 0, 2 * slots_all // lanes)

        @pl.loop(0, tiles)
        def _(t):
            cols = pl.ds(pl.multiple_of(t * tile_w, tile_w), tile_w)
            total = partial_tile(first, size, me, t)
            golden = choose(chosen, targets_ref, cols)

            @pl.when(me > 0)
            def _():
                wait_for(slots.at[me, t, where], rs_recv.at[k, me, t])

            @pl.when(me < last)
            def _():
                wait_for(slots.at[n, t, where], rs_recv.at[k, n, t])

            total += jnp.where(has_left, slots[me, t, where].astype(F32), 0.0)
            total += jnp.where(has_right, slots[n, t, where].astype(F32), 0.0)
            differ = jnp.clip(total - golden, -1.0, 1.0)
            grad = (differ * weight).astype(BF16)
            joined[where] += lax.dot_general(
                grad, pout_ref[:, cols], (((1,), (1,)), ((), ())), preferred_element_type=F32
            )

        @pl.when(me != keeper(k))
        def _():
            part_copy(k, first, size).start()

    @pl.loop(0, 2)
    def _(m):
        send_own(m)

    pair_copy(0, clips_ref).start()

    def prepare(k):
        first = sum(sizes[:k])

        @pl.loop(first, first + sizes[k])
        def _(m):
            later_table(m)

        if k == 1:
            wait_for(clips_ref.at[1 - core], pair_recv.at[0])
        pack_later(k, first, sizes[k])

    prepare(1)
    forward(1)
    send_own(2)
    prepare(2)
    forward(2)
    send_own(3)
    load_targets.wait()
    pair_copy(1, targets_ref).start()
    for k in range(3, steps):
        prepare(k)

    @pl.loop(3, 2 + last)
    def _(m):
        gather_step(m)

    loads[0].wait()
    order_row = lax.broadcasted_iota(jnp.int32, (proj, proj), 0)
    order_col = lax.broadcasted_iota(jnp.int32, (proj, proj), 1)
    half = proj // 2
    wanted = jnp.where(order_row < half, 2 * order_row, 2 * (order_row - half) + 1)
    shuffle = jnp.where(order_col == wanted, 1.0, 0.0).astype(BF16)
    pin_ref[:proj, :] = jnp.dot(shuffle, pin_raw[...], preferred_element_type=F32).astype(BF16)

    hidden_tiles = hidden_part // tile

    @pl.loop(0, steps + last)
    def _(k):
        upto = 2 * (k + 1) + last

        def more(i):
            @pl.when(upto + i < pieces + last)
            def _():
                gather_step(upto + i)

        @pl.when(k == 0)
        def _():
            loads[1].wait()
            loads[2].wait()

        def make_hidden(k, first, size):
            @pl.loop(0, hidden_tiles)
            def _(t):
                hidden_tile(first, size, t)

            join_left(first, size)

        by_size(k, make_hidden)

        @pl.when(k == steps - 1)
        def _():
            load_hessian.start()
            load_tests.start()

        @pl.when(k == 0)
        def _():
            for load in loads[3:]:
                load.wait()
            wait_for(targets_ref.at[1 - core], pair_recv.at[1])

        more(0)

        def send_right(k, first, size):
            @pl.loop(0, last - me)
            def _(i):
                add_and_send(0, k, first, size, last - i)

        by_size(k - me, send_right)

        def send_left(k, first, size):
            @pl.loop(0, me)
            def _(d):
                add_and_send(1, k, first, size, d)

        by_size(k - (last - me), send_left)
        by_size(k - last, finish)
        more(1)

    pair_start = my_clip - core

    def factor_copy(h, c):
        return pltpu.make_async_remote_copy(
            src_ref=factor.at[h, c],
            dst_ref=landed_factor.at[core, me],
            send_sem=fa_send.at[h, c],
            recv_sem=fa_recv.at[core, me],
            device_id={"clip": pair_start + h, "tensor": c},
            device_id_type=MESH,
        )

    def other_factors(act):
        @pl.loop(0, 2)
        def _(h):
            @pl.loop(0, count)
            def _(c):
                @pl.when((h != core) | (c != me))
                def _():
                    act(h, c)

    def add_product(k, first, size):
        held = pl.ds(0, size * rows)
        total = joined[span(first, size)]

        @pl.loop(0, n)
        def _(j):
            @pl.when(j != me)
            def _():
                wait_for(parts.at[k // n, j, held], own_recv.at[k // n, j])

        parts[k // n, me, held] = total
        total = parts[k // n, 0, held]
        for j in range(1, n):
            total += parts[k // n, j, held]
        lane = lax.broadcasted_iota(jnp.int32, total.shape, 1)
        right = jnp.where(lane < proj, pltpu.roll(total, proj, 1), total)
        owner = owner_ref[span(first, size)]
        product[...] += jnp.dot(
            total.T[:proj],
            jnp.concatenate(
                [jnp.where(owner == i, right, 0.0) for i in range(both_count)], axis=1
            ),
            precision=lax.Precision.HIGHEST,
            preferred_element_type=F32,
        )

    def is_keeper(z):
        return (z + n - shift) % n < steps

    @pl.when(is_keeper(me))
    def _():
        product[...] = jnp.zeros_like(product)
        for i in range(parts.shape[0]):
            by_size(kept + i * n, add_product)
        low = lax.broadcasted_iota(jnp.int32, (half, 2 * proj), 1) < proj
        for i in range(both_count):
            cols = slice(i * 2 * proj, (i + 1) * 2 * proj)
            factor[i // count, i % count] = jnp.where(
                low, product[:half, cols], product[half:, cols]
            )
        other_factors(lambda h, c: factor_copy(h, c).start())

    def sketch_copy(c, z):
        return pltpu.make_async_remote_copy(
            src_ref=blocks_out.at[c],
            dst_ref=landed_sketch.at[my_clip * count + me],
            send_sem=sk_send.at[c, z],
            recv_sem=sk_recv.at[my_clip * count + me],
            device_id={"clip": c, "tensor": z},
            device_id_type=MESH,
        )

    def every_other(act):
        @pl.loop(0, nc)
        def _(c):
            @pl.loop(0, n)
            def _(z):
                @pl.when((c != my_clip) | (z != me))
                def _():
                    act(c, z)

    @pl.when(me < count)
    def _():
        @pl.when(is_keeper(me))
        def _():
            landed_factor[core, me] = factor[core, me]

        if steps < n:
            @pl.loop(0, n)
            def _(z):
                @pl.when(jnp.logical_not(is_keeper(z)))
                def _():
                    landed_factor[0, z] = jnp.zeros_like(landed_factor[0, z])
                    landed_factor[1, z] = jnp.zeros_like(landed_factor[1, z])

        @pl.loop(0, 2)
        def _(h):
            @pl.loop(0, n)
            def _(z):
                @pl.when(((h != core) | (z != me)) & is_keeper(z))
                def _():
                    wait_for(landed_factor.at[h, z], fa_recv.at[h, z])

        total = landed_factor[0, 0]
        for z in range(1, 2 * n):
            total += landed_factor[z // n, z % n]
        total = total.astype(BF16).astype(F32)
        for c in range(nc):
            blocks_out[c] = total[c * per_block : (c + 1) * per_block]
        every_other(lambda c, z: sketch_copy(c, z).start())
        landed_sketch[my_clip * count + me] = blocks_out[my_clip]

    @pl.loop(0, nc)
    def _(c):
        @pl.loop(0, count)
        def _(z):
            @pl.when((c != my_clip) | (z != me))
            def _():
                wait_for(landed_sketch.at[c * count + z], sk_recv.at[c * count + z])

    def partial_copy(c):
        return pltpu.make_async_remote_copy(
            src_ref=partial,
            dst_ref=landed_partial.at[my_clip],
            send_sem=pp_send.at[c],
            recv_sem=pp_recv.at[my_clip],
            device_id={"clip": c, "tensor": me},
            device_id_type=MESH,
        )

    def block_copy(c, q):
        return pltpu.make_async_remote_copy(
            src_ref=blocks.at[c, q],
            dst_ref=landed_blocks.at[me],
            send_sem=bl_send.at[c, q],
            recv_sem=bl_recv.at[me],
            device_id={"clip": c, "tensor": my_clip * ratio + q},
            device_id_type=MESH,
        )

    def other_clips(act):
        @pl.loop(0, nc)
        def _(c):
            @pl.when(c != my_clip)
            def _():
                act(c)

    load_hessian.wait()
    stacked = jnp.concatenate([landed_sketch[:, r, :] for r in range(per_block)], axis=1)
    partial[...] = jnp.dot(
        stacked.astype(BF16), hessian_ref[...], preferred_element_type=F32
    ).astype(BF16)
    other_clips(lambda c: partial_copy(c).start())
    landed_partial[my_clip] = partial[...]
    load_tests.wait()
    other_clips(lambda c: wait_for(landed_partial.at[c], pp_recv.at[c]))
    precond = landed_partial[0].astype(F32)
    for c in range(1, nc):
        precond += landed_partial[c].astype(F32)
    scores = lax.dot_general(
        precond.astype(BF16),
        tests_ref[...],
        (((1,), (1,)), ((), ())),
        preferred_element_type=F32,
    )
    for c in range(nc):
        for q in range(ratio):
            blocks[c, q] = scores[
                c * count : (c + 1) * count, q * out_width : (q + 1) * out_width
            ]

    def elsewhere(c, q):
        return (c != my_clip) | (my_clip * ratio + q != me)

    @pl.loop(0, nc)
    def _(c):
        @pl.loop(0, ratio)
        def _(q):
            @pl.when(elsewhere(c, q))
            def _():
                block_copy(c, q).start()

            @pl.when(jnp.logical_not(elsewhere(c, q)))
            def _():
                landed_blocks[me] = blocks[c, q]

    pair_copy(0, clips_ref).wait_send()
    pair_copy(1, targets_ref).wait_send()

    @pl.loop(0, steps)
    def _(k):
        def wait_part(k, first, size):
            @pl.when(me != keeper(k))
            def _():
                part_copy(k, first, size).wait_send()

        by_size(k, wait_part)

    @pl.loop(0, n)
    def _(j):
        @pl.when((j <= me) & (me < last))
        def _():
            wait_for(tok.at[j], ag_send.at[0, j])

        @pl.when((j >= me) & (me > 0))
        def _():
            wait_for(tok.at[j], ag_send.at[1, j])

        @pl.when(j != me)
        def _():
            wait_for(slots.at[j], rs_send.at[j])

    @pl.when(is_keeper(me))
    def _():
        other_factors(lambda h, c: factor_copy(h, c).wait_send())

    @pl.when(me < count)
    def _():
        every_other(lambda c, z: sketch_copy(c, z).wait_send())

    other_clips(lambda c: partial_copy(c).wait_send())

    holds_own = (me >= my_clip * ratio) & (me < (my_clip + 1) * ratio)

    @pl.loop(0, n)
    def _(z):
        @pl.when((z != me) | jnp.logical_not(holds_own))
        def _():
            wait_for(landed_blocks.at[z], bl_recv.at[z])

    total = landed_blocks[0]
    for z in range(1, n):
        total += landed_blocks[z]
    out_ref[...] = total

    @pl.loop(0, nc)
    def _(c):
        @pl.loop(0, ratio)
        def _(q):
            @pl.when(elsewhere(c, q))
            def _():
                block_copy(c, q).wait_send()


def agree_kernel(
    capacities, parts_n, nc, lengths_ref, index_ref, pair_ref, landed, send_sem, recv_sem
):
    my_clip = lax.axis_index("clip")
    mine = lax.axis_index("parts") * nc + my_clip
    count = lengths_ref.shape[0]
    groups = parts_n * nc

    def others(act):
        @pl.loop(0, parts_n)
        def _(y):
            @pl.loop(0, nc)
            def _(c):
                @pl.when(y * nc + c != mine)
                def _():
                    act(y, c)

    barrier = pltpu.get_barrier_semaphore()
    others(
        lambda y, c: pl.semaphore_signal(
            barrier, inc=1, device_id={"parts": y, "clip": c}, device_id_type=MESH
        )
    )
    sublane = lax.broadcasted_iota(jnp.int32, landed.shape[1:], 0)
    tile = jnp.zeros(landed.shape[1:], jnp.int32)
    for i in range(count):
        tile = jnp.where(sublane == i, lengths_ref[i], tile)
    landed[mine] = tile
    pl.semaphore_wait(barrier, groups - 1)

    def lengths_copy(y, c):
        return pltpu.make_async_remote_copy(
            src_ref=landed.at[mine],
            dst_ref=landed.at[mine],
            send_sem=send_sem.at[y * nc + c],
            recv_sem=recv_sem.at[mine],
            device_id={"parts": y, "clip": c},
            device_id_type=MESH,
        )

    others(lambda y, c: lengths_copy(y, c).start())
    others(
        lambda y, c: wait_for(landed.at[y * nc + c], recv_sem.at[y * nc + c])
    )
    most = jnp.zeros((1, landed.shape[2]), jnp.int32)
    for g in range(0, groups, 2):
        pair = landed[g] + landed[g + 1]
        total = pair[0:1]
        for i in range(1, count):
            total = total + pair[i : i + 1]
        most = jnp.maximum(most, total)
    index = jnp.zeros_like(most)
    for capacity in capacities[:-1]:
        index = index + jnp.where(most > 2 * capacity, 1, 0)
    index_ref[0] = jnp.max(index)
    start = mine - my_clip % 2
    pair_ref[0:count] = landed[start, 0:count]
    pair_ref[count:] = landed[start + 1, 0:count]
    others(lambda y, c: lengths_copy(y, c).wait_send())


def agree(capacities, parts_n, nc, lengths):
    count = lengths.shape[0]
    groups = parts_n * nc
    return pl.pallas_call(
        functools.partial(agree_kernel, capacities, parts_n, nc),
        out_shape=(
            jax.ShapeDtypeStruct((1,), jnp.int32),
            jax.ShapeDtypeStruct((2 * count, 128), jnp.int32),
        ),
        in_specs=[pl.BlockSpec(memory_space=pltpu.SMEM)],
        out_specs=(
            pl.BlockSpec(memory_space=pltpu.SMEM),
            pl.BlockSpec(memory_space=pltpu.VMEM),
        ),
        scratch_shapes=[
            pltpu.VMEM((groups, 8, 128), jnp.int32),
            pltpu.SemaphoreType.DMA((groups,)),
            pltpu.SemaphoreType.DMA((groups,)),
        ],
        compiler_params=pltpu.CompilerParams(collective_id=0, has_side_effects=True),
        name="agree",
    )(lengths)


def make_call(nc, n, sizes, rows, collective_id, args):
    clips, targets, lengths, gate, up, down, pin, pout, hessian, tests = args
    slots_all, width = clips.shape
    both_count = lengths.shape[0]
    count = both_count // 2
    hidden_part = gate.shape[1]
    proj = pin.shape[0]
    both = 2 * proj
    depth, columns = hessian.shape
    ratio = n // nc
    out_width = tests.shape[0] // ratio
    tile = 256 if hidden_part % 256 == 0 else hidden_part
    tile_w = 256 if width % 256 == 0 else width
    ahead = 1
    steps, pieces = len(sizes), 2 * len(sizes)
    total = sum(sizes) * rows
    rounds = -(-steps // n)
    vmem = pl.BlockSpec(memory_space=pltpu.VMEM)
    hbm = pl.BlockSpec(memory_space=pltpu.HBM)
    dma = pltpu.SemaphoreType.DMA
    tiles = width // tile_w
    return pl.pallas_call(
        functools.partial(scores_kernel, nc, n, sizes, rows, tile, ahead),
        out_shape=jax.ShapeDtypeStruct((count, out_width), F32),
        in_specs=[hbm, hbm, vmem] + [hbm] * 7,
        out_specs=vmem,
        scratch_shapes=[
            pltpu.VMEM((2, *clips.shape), BF16),
            pltpu.VMEM((2, *targets.shape), BF16),
            pltpu.VMEM((total, 128), jnp.int32),
            pltpu.VMEM((total, 128), jnp.int32),
            pltpu.VMEM((total, 128), F32),
            pltpu.VMEM(pin.shape, BF16),
            pltpu.VMEM((both, hidden_part), BF16),
            pltpu.VMEM((both, width), BF16),
            pltpu.VMEM(gate.shape, BF16),
            pltpu.VMEM(up.shape, BF16),
            pltpu.VMEM(down.shape, BF16),
            pltpu.VMEM((n, total, width), BF16),
            pltpu.VMEM((n + 1, tiles, total, tile_w), BF16),
            pltpu.VMEM((total, hidden_part), BF16),
            pltpu.VMEM((total, both), F32),
            pltpu.VMEM((rounds, n, max(sizes) * rows, both), F32),
            pltpu.VMEM((proj, both_count * both), F32),
            pltpu.VMEM((2, count, proj // 2, both), F32),
            pltpu.VMEM((2, n, proj // 2, both), F32),
            pltpu.VMEM((nc, depth // both, both), F32),
            pltpu.VMEM((nc * count, depth // both, both), F32),
            pltpu.VMEM((nc * count, columns), BF16),
            pltpu.VMEM((nc, nc * count, columns), BF16),
            pltpu.VMEM((nc, ratio, count, out_width), F32),
            pltpu.VMEM((n, count, out_width), F32),
            dma((9,)),
            dma((2,)),
            dma((2,)),
            dma((2, n)),
            dma((pieces, n)),
            dma((n,)),
            dma((steps, n + 1, tiles)),
            dma((steps,)),
            dma((rounds, n)),
            dma((2, count)),
            dma((2, n)),
            dma((nc, n)),
            dma((nc * count,)),
            dma((nc,)),
            dma((nc,)),
            dma((nc, ratio)),
            dma((n,)),
        ],
        compiler_params=pltpu.CompilerParams(
            collective_id=collective_id,
            has_side_effects=True,
            vmem_limit_bytes=63 * 1024 * 1024,
        ),
        cost_estimate=pl.CostEstimate(
            flops=6 * total * hidden_part * width * n,
            bytes_accessed=2 * 3 * hidden_part * width * n,
            transcendentals=total * hidden_part,
        ),
        name=f"influence_{total}",
    )


def on_device(parts_n, nc, n, *args):
    clips, targets, lengths = args[:3]
    count, clip_rows, width = clips.shape
    slots_all = count * clip_rows
    rows = 16
    full = slots_all // (4 * rows)
    plans = [(5, 6, 6, 5), (6, 6, 6, 6), (6, 7, 7, 6), (full,) * 4]
    capacities = [sum(sizes) * rows for sizes in plans]
    index, pair_lengths = agree(capacities, parts_n, nc, lengths)
    flat = (
        clips.reshape(slots_all, width),
        targets.reshape(slots_all, width),
        pair_lengths,
        *args[3:],
    )
    calls = [
        make_call(nc, n, sizes, rows, 1 + i, flat)
        for i, sizes in enumerate(plans)
    ]
    return lax.switch(index[0], calls, *flat)


def solution(mesh):
    in_specs = (
        P(("parts", "clip"), None, "tensor"),
        P(("parts", "clip"), None, "tensor"),
        P(("parts", "clip")),
        P(None, "tensor"),
        P(None, "tensor"),
        P("tensor", None),
        P(None, "tensor"),
        P(),
        P("clip", "tensor"),
        P("clip", "tensor"),
    )
    out_specs = P(("parts", "clip"), "tensor")
    return jax.shard_map(
        functools.partial(
            on_device, mesh.shape["parts"], mesh.shape["clip"], mesh.shape["tensor"]
        ),
        mesh=mesh,
        in_specs=in_specs,
        out_specs=out_specs,
        check_vma=False,
    )
```
